32 devices in a mesh: ctx: 16 (over z, y, core), sec: 2 (over x).
Axes of the slice: x: 2, y: 2, z: 4, core: 2. Of those that a mesh axis runs over, the one named last changes fastest.
Arguments:
- query_nope: bfloat16 [1024, 8192], P('ctx', 'sec'), may hold values from -6 to 6
- query_rope: bfloat16 [1024, 4096], P('ctx', 'sec'), may hold values from -8 to 8
- key_latent: bfloat16 [1024, 512], P('ctx'), may hold values from -6 to 6
- key_rope: bfloat16 [1024, 64], P('ctx'), may hold values from -8 to 8
- key_up: bfloat16 [64, 512, 128], P('sec'), may hold values from -0.25 to 0.25
- value_up: bfloat16 [64, 512, 128], P('sec'), may hold values from -1 to 1
- routed_tokens: bfloat16 [4096, 7168], P(('ctx', 'sec')), may hold values from -6 to 6
- expert_ids: int32 [4096, 8], P(('ctx', 'sec')), may hold values from 0 to 255, as said below
- expert_gates: float32 [4096, 8], P(('ctx', 'sec')), may hold values from 0.2 to 2
- gate_weight: bfloat16 [7168, 8192], P(None, ('ctx', 'sec')), may hold values from -0.0625 to 0.0625
- up_weight: bfloat16 [7168, 8192], P(None, ('ctx', 'sec')), may hold values from -0.0625 to 0.0625
- down_weight: bfloat16 [8192, 7168], P(('ctx', 'sec')), may hold values from -0.125 to 0.125
Outputs:
- attention_out: bfloat16 [1024, 8192], P('ctx', 'sec')
- routed_out: bfloat16 [4096, 7168], P(('ctx', 'sec'))
The draws below stay inside these ranges and needn't reach their ends.
Inputs may be any that keep to these rules, and one draw needn't show every extreme that they name: `expert_ids`: each row names 8 different experts, at most one of them below 4. Within each aligned block of 128 rows (the rows of one device) no expert below 4 is named more than 4 times, and in every draw one expert below 4 is named exactly 4 times in every block.
All inputs are finite; a program needn't handle non-finite values.
Results may differ from the reference program's by a relative error of at most 0.008.
Values may be sent and summed in bfloat16 or wider, within the bound.
A program may use at most 192 MiB of HBM per device.

```python
import jax
import jax.numpy as jnp
from jax import lax

D = 7168
FF = 2048
EXPERTS = 256
TOPK = 8
LAT = 512
ROPE = 64
NOPE = 128
VDIM = 128
HEADS = 64
CAP = 4
MTOK_DEV = 128
EXP_ROUND = 4
SEQ = 1024
MTOKENS = 4096
ROUND_FF = 8192
N_CTX = 16
N_SEC = 2


def draw_query_rope(key, part):
    array_shape = (SEQ, HEADS * ROPE)
    values = jnp.clip(jax.random.normal(jax.random.fold_in(key, 1), array_shape, jnp.float32), -6.0, 6.0)
    return values.astype(jnp.bfloat16)


def draw_key_rope(key, part):
    array_shape = (SEQ, ROPE)
    values = jnp.clip(jax.random.normal(jax.random.fold_in(key, 2), array_shape, jnp.float32), -6.0, 6.0)
    return values.astype(jnp.bfloat16)


def draw_expert_ids(key, part):
    block_count = MTOKENS // MTOK_DEV
    outside_count = EXPERTS - EXP_ROUND
    scores = jax.random.randint(jax.random.fold_in(key, 1), (MTOKENS, outside_count), 0, 1 << 20)
    scores = scores * outside_count + jnp.arange(outside_count, dtype=jnp.int32)[None, :]
    picked = lax.top_k(scores, TOPK)[1].astype(jnp.int32) + EXP_ROUND
    levels = jax.random.randint(jax.random.fold_in(key, 2), (EXP_ROUND,), 1, 5)
    hot_expert = jax.random.randint(jax.random.fold_in(key, 3), (), 0, EXP_ROUND)
    counts = jax.random.randint(jax.random.fold_in(key, 4), (block_count, EXP_ROUND), 0, levels * CAP // 4 + 1)
    expert_range = jnp.arange(EXP_ROUND, dtype=jnp.int32)
    counts = jnp.where(expert_range[None, :] == hot_expert, CAP, counts)
    starts = jnp.cumsum(counts, axis=1) - counts
    block_keys = jax.random.split(jax.random.fold_in(key, 5), block_count)
    rank_rows = jax.vmap(lambda block_key: jax.random.permutation(block_key, MTOK_DEV))(block_keys)
    inside = (rank_rows[:, :, None] >= starts[:, None, :]) & (rank_rows[:, :, None] < (starts + counts)[:, None, :])
    member = jnp.any(inside, axis=2).reshape(MTOKENS)
    chosen = jnp.sum(jnp.where(inside, expert_range[None, None, :], 0), axis=2).reshape(MTOKENS)
    column = jax.random.randint(jax.random.fold_in(key, 6), (MTOKENS,), 0, TOPK)
    replace = member[:, None] & (jnp.arange(TOPK, dtype=jnp.int32)[None, :] == column[:, None])
    return jnp.where(replace, chosen[:, None], picked).astype(jnp.int32)


def steps_of(key, extent, shards, smallest, top_value):
    def one(dim, parts):
        heights = jax.random.uniform(jax.random.fold_in(jax.random.fold_in(key, 6), dim), (parts,), jnp.float32, smallest / len(shards), top_value / len(shards))
        return jnp.repeat(jnp.exp(heights), extent[dim] // parts).reshape((-1,) + (1,) * (len(extent) - dim - 1))

    gain = one(*shards[0])
    for cut in shards[1:]:
        gain = gain * one(*cut)
    return gain


def normal_values(rng, extent, width, limit, pieces=(), kind=jnp.bfloat16):
    array = jax.random.normal(rng, extent, jnp.float32) * width
    if len(pieces) > 0:
        array = steps_of(rng, extent, pieces, -0.22, 0.18) * array
    return jnp.clip(array, min=-limit, max=limit).astype(kind)


def setup_inputs(seed: int = 0) -> dict:
    streams_of = jax.random.split(jax.random.key(seed), 13)
    return {
        "query_nope": normal_values(streams_of[0], (SEQ, HEADS * NOPE), 1.0, 6.0, ((0, 16), (1, 2))),
        "query_rope": draw_query_rope(jax.random.fold_in(streams_of[12], 71), 0),
        "key_latent": normal_values(streams_of[2], (SEQ, LAT), 1.0, 6.0, ((0, 16),)),
        "key_rope": draw_key_rope(jax.random.fold_in(streams_of[12], 71), 0),
        "key_up": normal_values(streams_of[4], (HEADS, LAT, NOPE), LAT ** -0.5, 0.25, ((0, 2),)),
        "value_up": normal_values(streams_of[5], (HEADS, LAT, VDIM), (LAT // 16) ** -0.5, 1.0, ((0, 2),)),
        "routed_tokens": normal_values(streams_of[6], (MTOKENS, D), 1.0, 6.0, ((0, 32),)),
        "expert_ids": draw_expert_ids(jax.random.fold_in(streams_of[12], 71), 0),
        "expert_gates": jnp.clip(0.2 + 1.8 * jax.random.uniform(streams_of[8], (MTOKENS, TOPK), jnp.float32) ** steps_of(streams_of[8], (MTOKENS, TOPK), ((0, 32),), -0.2, 0.2), 0.2, 2.0),
        "gate_weight": normal_values(streams_of[9], (D, ROUND_FF), D ** -0.5, 0.0625, ((1, 32),)),
        "up_weight": normal_values(streams_of[10], (D, ROUND_FF), D ** -0.5, 0.0625, ((1, 32),)),
        "down_weight": normal_values(streams_of[11], (ROUND_FF, D), FF ** -0.5, 0.125, ((0, 32),)),
    }


def head_attention(query_latent, query_rotary, key_latent, key_rope, value_map):
    score_scale = (NOPE + ROPE) ** -0.5
    scores = jnp.dot(query_latent, key_latent.T, preferred_element_type=jnp.float32)
    scores = (scores + jnp.dot(query_rotary, key_rope.T, preferred_element_type=jnp.float32)) * score_scale
    places = jnp.arange(SEQ, dtype=jnp.int32)
    allowed = places[None, :] <= places[:, None]
    scores = jnp.where(allowed, scores, -jnp.inf)
    row_max = jnp.max(scores, axis=1, keepdims=True)
    exponent = jnp.where(allowed, jnp.exp(scores - row_max), 0.0)
    row_sum = jnp.sum(exponent, axis=1, keepdims=True)
    weights = exponent.astype(jnp.bfloat16)
    latent_out = (jnp.dot(weights, key_latent, preferred_element_type=jnp.float32) / row_sum).astype(jnp.bfloat16)
    return jnp.dot(latent_out, value_map, preferred_element_type=jnp.float32).astype(jnp.bfloat16)


def attention(query_nope, query_rope, key_latent, key_rope, key_up, value_up):
    nope_heads = query_nope.reshape(SEQ, HEADS, NOPE)
    rope_heads = query_rope.reshape(SEQ, HEADS, ROPE)

    def one_head(head_index):
        query_latent = jnp.dot(nope_heads[:, head_index, :], key_up[head_index].T, preferred_element_type=jnp.float32).astype(jnp.bfloat16)
        return head_attention(query_latent, rope_heads[:, head_index, :], key_latent, key_rope, value_up[head_index])

    per_head = lax.map(one_head, jnp.arange(HEADS, dtype=jnp.int32))
    return jnp.transpose(per_head, (1, 0, 2)).reshape(SEQ, HEADS * VDIM)


def routed_experts(routed_tokens, expert_ids, expert_gates, gate_weight, up_weight, down_weight):
    budget_rows = N_CTX * N_SEC * CAP
    slot_places = jnp.arange(budget_rows, dtype=jnp.int32)

    def one_expert(summed, expert):
        chosen = expert_ids == expert
        is_named = jnp.any(chosen, axis=1)
        coefficient = jnp.sum(jnp.where(chosen, expert_gates, 0.0), axis=1)
        named_count = jnp.sum(is_named.astype(jnp.int32))
        token_index = jnp.nonzero(is_named, size=budget_rows, fill_value=0)[0].astype(jnp.int32)
        picked_rows = routed_tokens[token_index]
        column_start = expert * FF
        gate_cols = lax.dynamic_slice_in_dim(gate_weight, column_start, FF, 1)
        up_cols = lax.dynamic_slice_in_dim(up_weight, column_start, FF, 1)
        down_rows = lax.dynamic_slice_in_dim(down_weight, column_start, FF, 0)
        gate_act = jnp.dot(picked_rows, gate_cols, preferred_element_type=jnp.float32)
        up_act = jnp.dot(picked_rows, up_cols, preferred_element_type=jnp.float32)
        hidden = (jax.nn.silu(gate_act) * up_act).astype(jnp.bfloat16)
        expert_out = jnp.dot(hidden, down_rows, preferred_element_type=jnp.float32)
        row_scale = jnp.where(slot_places < named_count, coefficient[token_index], 0.0)
        return summed.at[token_index].add(row_scale[:, None] * expert_out), None

    start_sum = jnp.zeros((MTOKENS, D), jnp.float32)
    summed, _ = lax.scan(one_expert, start_sum, jnp.arange(EXP_ROUND, dtype=jnp.int32))
    return summed.astype(jnp.bfloat16)


def reference(query_nope, query_rope, key_latent, key_rope, key_up, value_up, routed_tokens, expert_ids, expert_gates, gate_weight, up_weight, down_weight):
    attention_out = attention(query_nope, query_rope, key_latent, key_rope, key_up, value_up)
    routed_out = routed_experts(routed_tokens, expert_ids, expert_gates, gate_weight, up_weight, down_weight)
    return (attention_out, routed_out)
```

```python
import functools

import jax
import jax.numpy as jnp
from jax import lax
from jax.experimental import pallas as pl
from jax.experimental.pallas import tpu as pltpu
from jax.sharding import PartitionSpec as P

CAP = 4
SPLIT = 8
CHUNKS = 4
RCHUNKS = 8
PIECES = 4
LOG2E = 1.4426950408889634
MESH_ID = pl.DeviceIdType.MESH
F32 = jnp.float32
BF16 = jnp.bfloat16
NT = (((1,), (1,)), ((), ()))
scope = jax.named_scope


def kernel(
    dims,
    ids_hbm,
    gates_hbm,
    klat_hbm,
    krope_hbm,
    tok_hbm,
    qn_hbm,
    qr_hbm,
    ku_hbm,
    vu_hbm,
    gw_hbm,
    uw_hbm,
    dw_hbm,
    att_hbm,
    res_hbm,
    wmix_hbm,
    ids_ref,
    gates_ref,
    krope_ref,
    wmix,
    att_ref,
    tok,
    qn,
    qr,
    ku,
    vu,
    gw,
    uw,
    dw,
    qcat,
    keys,
    outg,
    zbuf,
    arr,
    acc,
    part,
    r1,
    s1,
    r2,
    s2,
    r3,
    rbuf,
    load_sem,
    store_sem,
    kz_send,
    kx_send,
    ky_send,
    kc_send,
    krecv,
    zsend,
    zrecv,
    asend,
    arecv,
    rsend,
    rrecv,
    bsend,
    brecv,
):
    groups, n_sec, rows, heads, lat, ropew, nope, hb = dims
    slots = groups * CAP
    width = tok.shape[1]
    cw = width // CHUNKS
    rw = width // RCHUNKS
    tokens = tok.shape[0]
    sent = lat + 2 * ropew
    ctx = lax.axis_index("ctx")
    sec = lax.axis_index("sec")
    me = ctx * n_sec + sec
    g = me // SPLIT
    m = lax.rem(me, SPLIT)
    bx = lax.rem(m, 2)
    bc = lax.rem(m // 2, 2)
    by = m // 4
    mx = m + 1 - 2 * bx
    mc = m + 2 - 4 * bc
    my = m + 4 - 8 * by
    mxy = mx + my - m

    def dev(group, member):
        index = group * SPLIT + member
        return (index // n_sec, lax.rem(index, n_sec))

    pending = []
    stores = []

    def rcopy(src, dst, ss, rs, target):
        return pltpu.make_async_remote_copy(
            src_ref=src, dst_ref=dst, send_sem=ss, recv_sem=rs,
            device_id=target, device_id_type=MESH_ID,
        )

    def send(src, dst, ss, rs, target):
        cp = rcopy(src, dst, ss, rs, target)
        cp.start()
        pending.append(cp)
        return cp

    def store(src, dst):
        cp = pltpu.make_async_copy(src, dst, store_sem.at[len(stores)])
        cp.start()
        stores.append(cp)

    nx, nc, ny = dev(g, mx), dev(g, mc), dev(g, my)
    others = [lax.rem(g + step, groups) for step in range(1, groups)]
    every = [g] + others

    barrier = pltpu.get_barrier_semaphore()
    for target in [dev(o, m) for o in others] + [nx, nc, ny]:
        pl.semaphore_signal(barrier, inc=1, device_id=target, device_id_type=MESH_ID)

    own_keys = keys.at[ctx]
    pairs = [
        (ids_hbm, ids_ref), (gates_hbm, gates_ref), (qn_hbm, qn), (qr_hbm, qr), (ku_hbm, ku),
        (gw_hbm, gw), (uw_hbm, uw), (dw_hbm, dw), (vu_hbm, vu),
        (klat_hbm, own_keys.at[:, pl.ds(0, lat)]), (krope_hbm, krope_ref),
    ]
    loads = [pltpu.make_async_copy(a, b, load_sem.at[i]) for i, (a, b) in enumerate(pairs)]
    l_ids, l_gates, l_qn, l_qr, l_ku, l_gw, l_uw, l_dw, l_vu, l_klat, l_krope = loads
    l_ids.start()
    l_gates.start()
    tok_loads = []
    for c in range(CHUNKS):
        cols = pl.ds(c * cw, cw)
        tok_loads.append(
            pltpu.make_async_copy(
                tok_hbm.at[:, cols], tok.at[:, cols], load_sem.at[len(loads) + c]
            )
        )
        tok_loads[c].start()
    l_klat.start()
    l_krope.start()

    part_rows = rows // 2

    def kpiece(shard, which):
        return keys.at[shard, pl.ds(pl.multiple_of(which * part_rows, part_rows), part_rows), pl.ds(0, sent)]

    def kwhole(shard):
        return keys.at[shard, :, pl.ds(0, sent)]

    def kshard(group, member):
        return (group * SPLIT + member) // n_sec

    def ksend(group, member, which, sem, target):
        shard = kshard(group, member)
        piece = kpiece(shard, which)
        send(piece, piece, sem, krecv.at[shard, which], target)

    def karrive(group, member, which):
        shard = kshard(group, member)
        piece = kpiece(shard, which)
        rcopy(piece, piece, kz_send.at[0], krecv.at[shard, which], nx).wait_recv()

    def ksend_whole(group, member, sem, target):
        shard = kshard(group, member)
        send(kwhole(shard), kwhole(shard), sem, krecv.at[shard, 0], target)

    def karrive_whole(group, member):
        shard = kshard(group, member)
        rcopy(kwhole(shard), kwhole(shard), kz_send.at[0], krecv.at[shard, 0], nx).wait_recv()

    with scope("a_sel"):
        lanes = wmix.shape[1]
        row = lax.broadcasted_iota(jnp.int32, (lanes, tokens), 0)
        slot = row & (slots - 1)
        expert = slot // CAP
        matches = jnp.zeros((lanes, tokens), F32)
        gate = jnp.zeros((lanes, tokens), F32)
        l_ids.wait()
        l_gates.wait()
        for load in (l_qn, l_qr, l_ku):
            load.start()
        for k in range(ids_ref.shape[0]):
            hit = ids_ref[k : k + 1, :] == expert
            matches = jnp.where(hit, 1.0, matches)
            gate = gate + jnp.where(hit, gates_ref[k : k + 1, :], 0.0)
        earlier = (
            lax.broadcasted_iota(jnp.int32, (tokens, tokens), 0)
            < lax.broadcasted_iota(jnp.int32, (tokens, tokens), 1)
        )
        rank = jnp.dot(
            matches.astype(BF16), jnp.where(earlier, 1.0, 0.0).astype(BF16), preferred_element_type=F32
        )
        chosen = jnp.where(rank == (slot & (CAP - 1)).astype(F32), matches, 0.0)
        picker = chosen[:slots].astype(BF16)

    with scope("b_pick"):
        for c in range(CHUNKS):
            tok_loads[c].wait()
            picked = jnp.dot(picker, tok[:, c * cw : (c + 1) * cw], preferred_element_type=F32)
            for e in range(groups):
                outg[c, e] = picked[e * CAP : (e + 1) * CAP].astype(BF16)
        l_klat.wait()
        l_krope.wait()
        own_keys[:, lat:sent] = jnp.concatenate([krope_ref[...], krope_ref[...]], axis=1)

    with scope("c_barrier"):
        pl.semaphore_wait(barrier, 3 + len(others))

    with scope("d_zsend"):
        for c in range(CHUNKS):
            for i, o in enumerate(others):
                send(outg.at[c, o], zbuf.at[c, g], zsend.at[c, i], zrecv.at[c, g], dev(o, m))
        ksend(g, m, bx, ky_send.at[0], ny)
        for i, o in enumerate(others):
            ksend_whole(g, m, kz_send.at[i], dev(o, m))

    with scope("e_wmix"):
        weight = chosen * gate
        w1 = weight.astype(BF16).astype(F32)
        w2 = (weight - w1).astype(BF16).astype(F32)
        w3 = weight - w1 - w2
        wmix[...] = jnp.where(
            row < slots, w1, jnp.where(row < 2 * slots, w2, jnp.where(row < 3 * slots, w3, 0.0))
        ).T.astype(BF16)
        store(wmix, wmix_hbm)

        maskw = keys.shape[2] - sent

        @pl.loop(0, keys.shape[0])
        def _(shard):
            key_place = shard * rows + lax.broadcasted_iota(jnp.int32, (rows, maskw), 0)
            query = lax.broadcasted_iota(jnp.int32, (rows, maskw), 1)
            hidden_key = (key_place > ctx * rows + query) & (query < rows)
            keys[shard, :, sent:] = jnp.where(hidden_key, -1e30, 0.0).astype(BF16)

        unit = jnp.where(
            lax.broadcasted_iota(jnp.int32, (rows, maskw), 0)
            == lax.broadcasted_iota(jnp.int32, (rows, maskw), 1),
            1.0,
            0.0,
        ).astype(BF16)

    with scope("f_loads"):
        l_qn.wait()
        l_qr.wait()
        l_ku.wait()
        for load in (l_gw, l_uw, l_dw, l_vu):
            load.start()

    def query_latents(first, last):
        with scope("ql"):
            @pl.loop(first, last)
            def _(p):
                rope = qr[:, pl.ds(pl.multiple_of(p * 2 * ropew, 2 * ropew), 2 * ropew)]
                low = lax.broadcasted_iota(jnp.int32, rope.shape, 1) < ropew
                for k in range(2):
                    h = p * 2 + k
                    q = qn[:, pl.ds(pl.multiple_of(h * nope, nope), nope)]
                    latent = lax.dot_general(q, ku[h], NT, preferred_element_type=F32)
                    place = pl.ds(pl.multiple_of(h * rows, rows), rows)
                    qcat[place, :lat] = latent.astype(BF16)
                    keep = low if k == 0 else jnp.logical_not(low)
                    qcat[place, lat:sent] = jnp.where(keep, rope.astype(F32), 0.0).astype(BF16)
                    qcat[place, sent:] = unit

    def spread(kind, member, c, target):
        piece = arr.at[c, member]
        send(piece, piece, asend.at[kind, c], arecv.at[c, member], target)

    def arrive(member, c):
        piece = arr.at[c, member]
        rcopy(piece, piece, asend.at[0, c], arecv.at[c, member], nx).wait_recv()

    def start_chunk(c):
        with scope("s%d" % c):
            for i, o in enumerate(others):
                rcopy(outg.at[c, o], zbuf.at[c, o], zsend.at[c, i], zrecv.at[c, o], dev(o, m)).wait_recv()
            zbuf[c, g] = outg[c, g]
            blocks = [zbuf[c, e].astype(F32) for e in range(groups)]
            arr[c, m] = jnp.concatenate(blocks, axis=0).astype(BF16)
            spread(0, m, c, nx)
            spread(1, m, c, ny)
            spread(2, m, c, nc)

    def forward_chunk(c):
        with scope("fw%d" % c):
            arrive(mx, c)
            if c % 2 == 0:
                spread(3, mx, c, ny)
            spread(4, mx, c, nc)
            arrive(my, c)
            if c % 2 == 1:
                spread(3, my, c, nx)
            spread(5, my, c, nc)

    count = SPLIT * slots

    def finish_chunk(c):
        with scope("fin%d" % c):
            arrive(mxy, c)
            spread(6, mxy, c, nc)

    def gate_up(c):
        with scope("guw%d" % c):
            for member in (mc, mx + mc - m, my + mc - m, mxy + mc - m):
                arrive(member, c)
        with scope("gu%d" % c):
            x = arr[c].reshape(count, cw)
            g_part = jnp.dot(x, gw[c * cw : (c + 1) * cw], preferred_element_type=F32)
            u_part = jnp.dot(x, uw[c * cw : (c + 1) * cw], preferred_element_type=F32)
            if c == 0:
                acc[0] = g_part
                acc[1] = u_part
            else:
                acc[0] += g_part
                acc[1] += u_part

    def kx_own():
        with scope("kxo"):
            karrive(g, my, bx)
            ksend(g, my, bx, kx_send.at[0], nx)

    def ky_step():
        with scope("ky"):
            for i, o in enumerate(others):
                karrive_whole(o, m)
                ksend(o, m, bx, ky_send.at[i + 1], ny)

    def kx_step():
        with scope("kx"):
            for i, o in enumerate(others):
                karrive(o, my, bx)
                ksend(o, my, bx, kx_send.at[i + 1], nx)

    def kc_step():
        with scope("kc"):
            for i, o in enumerate(every):
                ksend_whole(o, m, kc_send.at[i, 0], nc)
            for i, o in enumerate(every):
                karrive(o, my, 1 - bx)
                ksend_whole(o, my, kc_send.at[i, 1], nc)

    def key_wait():
        with scope("kw"):
            for o in every:
                for member in (mc, my + mc - m):
                    karrive_whole(o, member)

    pairs_n = heads // 2

    def ql(a, b):
        query_latents(a * pairs_n // 8, b * pairs_n // 8)

    ql(0, 3)
    start_chunk(0)
    kx_own()
    ql(3, 4)
    start_chunk(1)
    ql(4, 5)
    forward_chunk(0)
    start_chunk(2)
    ql(5, 6)
    forward_chunk(1)
    start_chunk(3)
    finish_chunk(0)
    ql(6, 7)
    forward_chunk(2)
    l_gw.wait()
    l_uw.wait()
    finish_chunk(1)
    gate_up(0)
    forward_chunk(3)
    ky_step()
    finish_chunk(2)
    gate_up(1)
    ql(7, 8)
    finish_chunk(3)
    gate_up(2)
    kx_step()
    gate_up(3)
    with scope("act"):
        gate_act = acc[0]
        hidden = (gate_act / (1.0 + jnp.exp(-gate_act)) * acc[1]).astype(BF16)
        l_dw.wait()

    c1, c2, c3 = [], [], []

    def down(c):
        value = jnp.dot(hidden, dw[:, c * rw : (c + 1) * rw], preferred_element_type=F32)
        part[c] = value.astype(BF16).reshape(2, 2, 2, slots, rw)
        c1.append(send(part.at[c, :, 1 - bc], r1.at[c], rsend.at[0, c], rrecv.at[0, c], nc))

    def sum_cores(c):
        with scope("sc%d" % c):
            c1[c].wait_recv()
            for a in range(2):
                for b in range(2):
                    s1[c, a, b] = (part[c, a, bc, b].astype(F32) + r1[c, a, b].astype(F32)).astype(BF16)
            src = s1.at[c, :, 1 - bx] if c % 2 == 0 else s1.at[c, 1 - by]
            c2.append(send(src, r2.at[c], rsend.at[1, c], rrecv.at[1, c], nx if c % 2 == 0 else ny))

    def sum_first(c):
        with scope("sf%d" % c):
            c2[c].wait_recv()
            for a in range(2):
                mine = s1[c, a, bx] if c % 2 == 0 else s1[c, by, a]
                s2[c, a] = (mine.astype(F32) + r2[c, a].astype(F32)).astype(BF16)
            keep = by if c % 2 == 0 else bx
            c3.append(send(s2.at[c, 1 - keep], r3.at[c], rsend.at[2, c], rrecv.at[2, c],
                           ny if c % 2 == 0 else nx))

    def sum_second(c):
        with scope("ss%d" % c):
            c3[c].wait_recv()
            keep = by if c % 2 == 0 else bx
            total = s2[c, keep].astype(F32) + r3[c].astype(F32)
            for e in range(groups):
                rbuf[c, e] = total[e * CAP : (e + 1) * CAP].astype(BF16)
            for i, o in enumerate(others):
                send(rbuf.at[c, o], res_hbm.at[c, g], bsend.at[c, i], brecv.at[c, g], dev(o, m))
            store(rbuf.at[c, g], res_hbm.at[c, g])

    seq = keys.shape[0] * keys.shape[1]
    block = hb * rows
    scale = (nope + ropew) ** -0.5 * LOG2E
    nb = heads // hb
    vdim = vu.shape[2]

    def attend(a, b):
        first, last = a * nb // 8, b * nb // 8
        with scope("att%d" % a):
            @pl.loop(first, last)
            def _(b):
                q = qcat[pl.ds(pl.multiple_of(b * block, block), block)]
                kk = keys[...].reshape(seq, keys.shape[2])
                score = lax.dot_general(q, kk, NT, preferred_element_type=F32)
                top = jnp.max(score, axis=1, keepdims=True)
                expo = jnp.exp2((score - top) * scale)
                total = jnp.sum(expo, axis=1, keepdims=True)
                mixed = jnp.dot(expo.astype(BF16), kk[:, :lat], preferred_element_type=F32)
                mixed = (mixed / total).astype(BF16)
                for k in range(hb):
                    h = b * hb + k
                    value = jnp.dot(
                        mixed[k * rows : (k + 1) * rows], vu[h], preferred_element_type=F32
                    )
                    att_ref[:, pl.ds(pl.multiple_of(h * vdim, vdim), vdim)] = value.astype(BF16)

            cols = pl.ds(first * hb * vdim, (last - first) * hb * vdim)
            store(att_ref.at[:, cols], att_hbm.at[:, cols])

    def pair(fn, k):
        fn(2 * k)
        fn(2 * k + 1)

    with scope("down"):
        for c in range(RCHUNKS):
            down(c)
    pair(sum_cores, 0)
    pair(sum_cores, 1)
    kc_step()
    pair(sum_first, 0)
    pair(sum_cores, 2)
    with scope("vuw"):
        l_vu.wait()
    key_wait()
    attend(0, 1)
    pair(sum_first, 1)
    pair(sum_cores, 3)
    pair(sum_second, 0)
    attend(1, 2)
    pair(sum_first, 2)
    pair(sum_second, 1)
    attend(2, 3)
    pair(sum_first, 3)
    pair(sum_second, 2)
    attend(3, 5)
    pair(sum_second, 3)
    attend(5, 8)

    with scope("z_res"):
        for c in range(RCHUNKS):
            for i, o in enumerate(others):
                rcopy(rbuf.at[c, o], res_hbm.at[c, o], bsend.at[c, i], brecv.at[c, o], dev(o, m)).wait_recv()
    with scope("z_sends"):
        for cp in pending:
            cp.wait_send()
        for cp in stores:
            cp.wait()


def finish(res_hbm, wmix_hbm, att_hbm, rout_hbm, out_hbm, res, wmix, att, rout, sem):
    chunks, groups, _, cw = res.shape
    step = chunks // PIECES
    w_load = pltpu.make_async_copy(wmix_hbm, wmix, sem.at[0])
    w_load.start()
    loads = []
    for p in range(PIECES):
        piece = pl.ds(p * step, step)
        loads.append(pltpu.make_async_copy(res_hbm.at[piece], res.at[piece], sem.at[1 + p]))
        loads[p].start()
    a_load = pltpu.make_async_copy(att_hbm, att, sem.at[1 + PIECES])
    a_load.start()
    w_load.wait()
    stores = []
    for p in range(PIECES):
        loads[p].wait()
        for c in range(p * step, (p + 1) * step):
            blocks = [res[c, e].astype(F32) for e in range(groups)]
            block_rows = jnp.concatenate(blocks, axis=0).astype(BF16)
            tall = jnp.concatenate([block_rows] * 3, axis=0)
            rout[:, c * cw : (c + 1) * cw] = jnp.dot(
                wmix[:, : tall.shape[0]], tall, preferred_element_type=F32
            ).astype(BF16)
        cols = pl.ds(p * step * cw, step * cw)
        stores.append(
            pltpu.make_async_copy(rout.at[:, cols], rout_hbm.at[:, cols], sem.at[2 + PIECES + p])
        )
        stores[p].start()
    a_load.wait()
    stores.append(pltpu.make_async_copy(att, out_hbm, sem.at[2 + 2 * PIECES]))
    stores[-1].start()
    for cp in stores:
        cp.wait()


def local(n_ctx, n_sec, qn, qr, klat, krope, ku, vu, tok, ids, gates, gw, uw, dw):
    devices = n_ctx * n_sec
    groups = devices // SPLIT
    slots = groups * CAP
    rows = qn.shape[0]
    heads, lat, nope = ku.shape
    ropew = krope.shape[1]
    tokens, width = tok.shape
    cw = width // CHUNKS
    rw = width // RCHUNKS
    kw = lat + 2 * ropew + 128
    hb = 4 if n_ctx * rows <= 2048 else 1
    lanes = -(-3 * slots // 128) * 128
    dims = (groups, n_sec, rows, heads, lat, ropew, nope, hb)
    a = pl.BlockSpec(memory_space=pl.ANY)
    dma = pltpu.SemaphoreType.DMA
    out_width = heads * vu.shape[2]
    att, res, wmix = pl.pallas_call(
        functools.partial(kernel, dims),
        out_shape=(
            jax.ShapeDtypeStruct((rows, out_width), BF16),
            jax.ShapeDtypeStruct((RCHUNKS, groups, CAP, rw), BF16),
            jax.ShapeDtypeStruct((tokens, lanes), BF16),
        ),
        in_specs=[a] * 12,
        out_specs=(a, a, a),
        scratch_shapes=[
            pltpu.VMEM(ids.shape[::-1], ids.dtype),
            pltpu.VMEM(gates.shape[::-1], gates.dtype),
            pltpu.VMEM(krope.shape, BF16),
            pltpu.VMEM((tokens, lanes), BF16),
            pltpu.VMEM((rows, out_width), BF16),
            pltpu.VMEM(tok.shape, BF16),
            pltpu.VMEM(qn.shape, BF16),
            pltpu.VMEM(qr.shape, BF16),
            pltpu.VMEM(ku.shape, BF16),
            pltpu.VMEM(vu.shape, BF16),
            pltpu.VMEM(gw.shape, BF16),
            pltpu.VMEM(uw.shape, BF16),
            pltpu.VMEM(dw.shape, BF16),
            pltpu.VMEM((heads * rows, kw), BF16),
            pltpu.VMEM((n_ctx, rows, kw), BF16),
            pltpu.VMEM((CHUNKS, groups, CAP, cw), BF16),
            pltpu.VMEM((CHUNKS, groups, CAP, cw), BF16),
            pltpu.VMEM((CHUNKS, SPLIT, slots, cw), BF16),
            pltpu.VMEM((2, SPLIT * slots, gw.shape[1]), F32),
            pltpu.VMEM((RCHUNKS, 2, 2, 2, slots, rw), BF16),
            pltpu.VMEM((RCHUNKS, 2, 2, slots, rw), BF16),
            pltpu.VMEM((RCHUNKS, 2, 2, slots, rw), BF16),
            pltpu.VMEM((RCHUNKS, 2, slots, rw), BF16),
            pltpu.VMEM((RCHUNKS, 2, slots, rw), BF16),
            pltpu.VMEM((RCHUNKS, slots, rw), BF16),
            pltpu.VMEM((RCHUNKS, groups, CAP, rw), BF16),
            dma((11 + CHUNKS,)),
            dma((1 + RCHUNKS + 8,)),
            dma((groups,)),
            dma((groups,)),
            dma((groups,)),
            dma((groups, 2)),
            dma((n_ctx, 2)),
            dma((CHUNKS, groups)),
            dma((CHUNKS, groups)),
            dma((7, CHUNKS)),
            dma((CHUNKS, SPLIT)),
            dma((3, RCHUNKS)),
            dma((3, RCHUNKS)),
            dma((RCHUNKS, groups)),
            dma((RCHUNKS, groups)),
        ],
        compiler_params=pltpu.CompilerParams(
            collective_id=0, has_side_effects=True, vmem_limit_bytes=67043328
        ),
    )(ids.T, gates.T, klat, krope, tok, qn, qr, ku, vu, gw, uw, dw)
    rout, att = pl.pallas_call(
        finish,
        out_shape=(jax.ShapeDtypeStruct(tok.shape, BF16), jax.ShapeDtypeStruct(att.shape, BF16)),
        in_specs=[a, a, a],
        out_specs=(a, a),
        scratch_shapes=[
            pltpu.VMEM(res.shape, BF16),
            pltpu.VMEM(wmix.shape, BF16),
            pltpu.VMEM(att.shape, BF16),
            pltpu.VMEM(tok.shape, BF16),
            dma((3 + 2 * PIECES,)),
        ],
    )(res, wmix, att)
    return att, rout


def solution(mesh):
    body = functools.partial(local, mesh.shape["ctx"], mesh.shape["sec"])
    both = ("ctx", "sec")
    return jax.shard_map(
        body,
        mesh=mesh,
        in_specs=(
            P("ctx", "sec"),
            P("ctx", "sec"),
            P("ctx", None),
            P("ctx", None),
            P("sec", None, None),
            P("sec", None, None),
            P(both, None),
            P(both, None),
            P(both, None),
            P(None, both),
            P(None, both),
            P(both, None),
        ),
        out_specs=(P("ctx", "sec"), P(both, None)),
        check_vma=False,
    )
```

```python
import functools

import jax
import jax.numpy as jnp
from jax import lax
from jax.experimental import pallas as pl
from jax.experimental.pallas import tpu as pltpu
from jax.sharding import PartitionSpec as P

CAP = 4
SPLIT = 8
CHUNKS = 4
RCHUNKS = 8
PIECES = 4
LOG2E = 1.4426950408889634
MESH_ID = pl.DeviceIdType.MESH
F32 = jnp.float32
BF16 = jnp.bfloat16
NT = (((1,), (1,)), ((), ()))
scope = jax.named_scope


def kernel(
    dims,
    ids_hbm,
    gates_hbm,
    klat_hbm,
    krope_hbm,
    tok_hbm,
    qn_hbm,
    qr_hbm,
    ku_hbm,
    vu_hbm,
    gw_hbm,
    uw_hbm,
    dw_hbm,
    att_hbm,
    res_hbm,
    wmix_hbm,
    ids_ref,
    gates_ref,
    krope_ref,
    wmix,
    att_ref,
    tok,
    qn,
    qr,
    ku,
    vu,
    gw,
    uw,
    dw,
    qcat,
    keys,
    outg,
    zbuf,
    arr,
    acc,
    part,
    r1,
    s1,
    r2,
    s2,
    r3,
    rbuf,
    load_sem,
    store_sem,
    send_sem,
    ksend,
    krecv,
    zrecv,
    arecv,
    rrecv,
    brecv,
):
    groups, n_sec, rows, heads, lat, ropew, nope, hb = dims
    slots = groups * CAP
    width = tok.shape[1]
    cw = width // CHUNKS
    rw = width // RCHUNKS
    tokens = tok.shape[0]
    sent = lat + 2 * ropew
    ctx = lax.axis_index("ctx")
    sec = lax.axis_index("sec")
    me = ctx * n_sec + sec
    g = me // SPLIT
    m = lax.rem(me, SPLIT)
    bx = lax.rem(m, 2)
    bc = lax.rem(m // 2, 2)
    by = m // 4
    mx = m + 1 - 2 * bx
    mc = m + 2 - 4 * bc
    my = m + 4 - 8 * by
    mxy = mx + my - m

    def dev(group, member):
        index = group * SPLIT + member
        return (index // n_sec, lax.rem(index, n_sec))


    def rcopy(src, dst, ss, rs, target):
        return pltpu.make_async_remote_copy(
            src_ref=src, dst_ref=dst, send_sem=ss, recv_sem=rs,
            device_id=target, device_id_type=MESH_ID,
        )

    def send(src, dst, kind, rs, target):
        rcopy(src, dst, send_sem.at[kind], rs, target).start()

    def received(like, rs):
        rcopy(like, like, send_sem.at[0], rs, nx).wait_recv()

    def store(src, dst, kind):
        pltpu.make_async_copy(src, dst, store_sem.at[kind]).start()

    nx, nc, ny = dev(g, mx), dev(g, mc), dev(g, my)
    others = [lax.rem(g + step, groups) for step in range(1, groups)]
    every = [g] + others

    barrier = pltpu.get_barrier_semaphore()
    for target in [dev(o, m) for o in others] + [nx, nc, ny]:
        pl.semaphore_signal(barrier, inc=1, device_id=target, device_id_type=MESH_ID)

    own_keys = keys.at[ctx]
    pairs = [
        (ids_hbm, ids_ref), (gates_hbm, gates_ref), (qn_hbm, qn), (qr_hbm, qr), (ku_hbm, ku),
        (gw_hbm, gw), (uw_hbm, uw), (dw_hbm, dw), (vu_hbm, vu),
        (klat_hbm, own_keys.at[:, pl.ds(0, lat)]), (krope_hbm, krope_ref),
    ]
    loads = [pltpu.make_async_copy(a, b, load_sem.at[i]) for i, (a, b) in enumerate(pairs)]
    l_ids, l_gates, l_qn, l_qr, l_ku, l_gw, l_uw, l_dw, l_vu, l_klat, l_krope = loads
    l_ids.start()
    l_gates.start()
    tok_loads = []
    for c in range(CHUNKS):
        cols = pl.ds(c * cw, cw)
        tok_loads.append(
            pltpu.make_async_copy(
                tok_hbm.at[:, cols], tok.at[:, cols], load_sem.at[len(loads) + c]
            )
        )
        tok_loads[c].start()
    l_klat.start()
    l_krope.start()

    def kwhole(shard):
        return keys.at[shard, :, pl.ds(0, sent)]

    def kshard(group, member):
        return (group * SPLIT + member) // n_sec

    def whole(group, member, way, s, target, rs=None):
        piece = kwhole(kshard(group, member))
        rcopy(piece, piece, ksend.at[way, s], krecv.at[way, s if rs is None else rs], target).start()

    up = dev(lax.rem(g + 1, groups), m)
    top_plane = groups - 1

    def guarded(s, fn):
        if s == 0:
            fn()
        else:
            pl.when(g >= s)(fn)

    def key_up(s, member, way):
        if s >= top_plane:
            return
        cond = g < top_plane if s == 0 else (g >= s) & (g < top_plane)

        @pl.when(cond)
        def _():
            whole(g - s, member, way, s, up, s + 1)

    def key_own():
        whole(g, m, 1, 0, ny)
        whole(g, m, 3, 0, nc)

    def key_pass(s, member, way):
        with scope("kp%d_%d" % (s, way)):
            if s == 0 and way == 0:
                key_up(0, m, 0)
                return

            @functools.partial(guarded, s)
            def _():
                received(kwhole(0), krecv.at[1 if s == 0 else way, s])

            key_up(s, member, way)

            @functools.partial(guarded, s)
            def _():
                whole(g - s, member, 3, s, nc)

    def key_a(s):
        key_pass(s, m, 0)

    def key_b(s):
        key_pass(s, my, 2)

    def key_w(s):
        with scope("kw%d" % s):
            @functools.partial(guarded, s)
            def _():
                received(keys.at[pl.ds(0, 2), :, pl.ds(0, sent)], krecv.at[3, s])

    with scope("a_sel"):
        lanes = wmix.shape[1]
        row = lax.broadcasted_iota(jnp.int32, (lanes, tokens), 0)
        slot = row & (slots - 1)
        expert = slot // CAP
        matches = jnp.zeros((lanes, tokens), F32)
        gate = jnp.zeros((lanes, tokens), F32)
        l_ids.wait()
        l_gates.wait()
        for load in (l_qn, l_qr, l_ku):
            load.start()
        for k in range(ids_ref.shape[0]):
            hit = ids_ref[k : k + 1, :] == expert
            matches = jnp.where(hit, 1.0, matches)
            gate = gate + jnp.where(hit, gates_ref[k : k + 1, :], 0.0)
        earlier = (
            lax.broadcasted_iota(jnp.int32, (tokens, tokens), 0)
            < lax.broadcasted_iota(jnp.int32, (tokens, tokens), 1)
        )
        rank = jnp.dot(
            matches.astype(BF16), jnp.where(earlier, 1.0, 0.0).astype(BF16), preferred_element_type=F32
        )
        chosen = jnp.where(rank == (slot & (CAP - 1)).astype(F32), matches, 0.0)
        picker = chosen[:slots].astype(BF16)

    with scope("b_pick"):
        for c in range(CHUNKS):
            tok_loads[c].wait()
            picked = jnp.dot(picker, tok[:, c * cw : (c + 1) * cw], preferred_element_type=F32)
            for e in range(groups):
                outg[c, e] = picked[e * CAP : (e + 1) * CAP].astype(BF16)
        l_klat.wait()
        l_krope.wait()
        own_keys[:, lat:sent] = jnp.concatenate([krope_ref[...], krope_ref[...]], axis=1)

    with scope("c_barrier"):
        pl.semaphore_wait(barrier, 3 + len(others))

    with scope("d_zsend"):
        for c in range(CHUNKS):
            for i, o in enumerate(others):
                send(outg.at[c, o], zbuf.at[c, g], 0, zrecv.at[c], dev(o, m))
        key_own()

    with scope("e_wmix"):
        weight = chosen * gate
        w1 = weight.astype(BF16).astype(F32)
        w2 = (weight - w1).astype(BF16).astype(F32)
        w3 = weight - w1 - w2
        wmix[...] = jnp.where(
            row < slots, w1, jnp.where(row < 2 * slots, w2, jnp.where(row < 3 * slots, w3, 0.0))
        ).T.astype(BF16)
        store(wmix, wmix_hbm, 0)

        maskw = keys.shape[2] - sent

        @pl.loop(0, keys.shape[0])
        def _(shard):
            key_place = shard * rows + lax.broadcasted_iota(jnp.int32, (rows, maskw), 0)
            query = lax.broadcasted_iota(jnp.int32, (rows, maskw), 1)
            hidden_key = (key_place > ctx * rows + query) & (query < rows)
            keys[shard, :, sent:] = jnp.where(hidden_key, -1e30, 0.0).astype(BF16)

        unit = jnp.where(
            lax.broadcasted_iota(jnp.int32, (rows, maskw), 0)
            == lax.broadcasted_iota(jnp.int32, (rows, maskw), 1),
            1.0,
            0.0,
        ).astype(BF16)

    per = SPLIT // n_sec
    with scope("zero"):
        for s in range(1, groups):
            @pl.when(g + s < groups)
            def _():
                keys[pl.ds((g + s) * per, per), :, :sent] = jnp.zeros((per, rows, sent), BF16)

    with scope("f_loads"):
        l_qn.wait()
        l_qr.wait()
        l_ku.wait()
        for load in (l_gw, l_uw, l_dw, l_vu):
            load.start()

    def query_latents(first, last):
        with scope("ql"):
            @pl.loop(first, last)
            def _(p):
                rope = qr[:, pl.ds(pl.multiple_of(p * 2 * ropew, 2 * ropew), 2 * ropew)]
                low = lax.broadcasted_iota(jnp.int32, rope.shape, 1) < ropew
                for k in range(2):
                    h = p * 2 + k
                    q = qn[:, pl.ds(pl.multiple_of(h * nope, nope), nope)]
                    latent = lax.dot_general(q, ku[h], NT, preferred_element_type=F32)
                    place = pl.ds(pl.multiple_of(h * rows, rows), rows)
                    qcat[place, :lat] = latent.astype(BF16)
                    keep = low if k == 0 else jnp.logical_not(low)
                    qcat[place, lat:sent] = jnp.where(keep, rope.astype(F32), 0.0).astype(BF16)
                    qcat[place, sent:] = unit

    def spread(member, c, way, target):
        piece = arr.at[c, member]
        send(piece, piece, 1, arecv.at[c, way], target)

    def arrive(c, way):
        received(arr.at[c, 0] if way < 3 else arr.at[c, pl.ds(0, 4)], arecv.at[c, way])

    def start_chunk(c):
        with scope("s%d" % c):
            received(zbuf.at[c, pl.ds(0, groups - 1)], zrecv.at[c])
            zbuf[c, g] = outg[c, g]
            blocks = [zbuf[c, e].astype(F32) for e in range(groups)]
            arr[c, m] = jnp.concatenate(blocks, axis=0).astype(BF16)
            spread(m, c, 0, nx)
            spread(m, c, 1, ny)
            spread(m, c, 3, nc)

    def forward_chunk(c):
        with scope("fw%d" % c):
            arrive(c, 0)
            if c % 2 == 0:
                spread(mx, c, 2, ny)
            spread(mx, c, 3, nc)
            arrive(c, 1)
            if c % 2 == 1:
                spread(my, c, 2, nx)
            spread(my, c, 3, nc)

    count = SPLIT * slots

    def finish_chunk(c):
        with scope("fin%d" % c):
            arrive(c, 2)
            spread(mxy, c, 3, nc)

    def gate_up(c):
        with scope("guw%d" % c):
            arrive(c, 3)
        with scope("gu%d" % c):
            x = arr[c].reshape(count, cw)
            g_part = jnp.dot(x, gw[c * cw : (c + 1) * cw], preferred_element_type=F32)
            u_part = jnp.dot(x, uw[c * cw : (c + 1) * cw], preferred_element_type=F32)
            if c == 0:
                acc[0] = g_part
                acc[1] = u_part
            else:
                acc[0] += g_part
                acc[1] += u_part

    pairs_n = heads // 2

    def ql(a, b):
        query_latents(a * pairs_n // 8, b * pairs_n // 8)

    seq = keys.shape[0] * keys.shape[1]
    block = hb * rows
    scale = (nope + ropew) ** -0.5 * LOG2E
    nb = heads // hb
    vdim = vu.shape[2]

    def attend(a, b):
        first, last = a * nb // 8, b * nb // 8
        with scope("att%d" % a):
            @pl.loop(first, last)
            def _(b):
                q = qcat[pl.ds(pl.multiple_of(b * block, block), block)]
                kk = keys[...].reshape(seq, keys.shape[2])
                score = lax.dot_general(q, kk, NT, preferred_element_type=F32)
                top = jnp.max(score, axis=1, keepdims=True)
                expo = jnp.exp2((score - top) * scale)
                total = jnp.sum(expo, axis=1, keepdims=True)
                mixed = jnp.dot(expo.astype(BF16), kk[:, :lat], preferred_element_type=F32)
                mixed = (mixed / total).astype(BF16)
                for k in range(hb):
                    h = b * hb + k
                    value = jnp.dot(
                        mixed[k * rows : (k + 1) * rows], vu[h], preferred_element_type=F32
                    )
                    att_ref[:, pl.ds(pl.multiple_of(h * vdim, vdim), vdim)] = value.astype(BF16)

            cols = pl.ds(first * hb * vdim, (last - first) * hb * vdim)
            store(att_ref.at[:, cols], att_hbm.at[:, cols], 2)

    def far(fn, first):
        for s in range(first, groups):
            fn(s)

    ql(0, 4)
    start_chunk(0)
    key_a(0)
    start_chunk(1)
    key_b(0)
    ql(4, 5)
    start_chunk(2)
    ql(5, 6)
    start_chunk(3)
    forward_chunk(0)
    ql(6, 7)
    key_a(1)
    forward_chunk(1)
    ql(7, 8)
    forward_chunk(2)
    key_b(1)
    forward_chunk(3)
    finish_chunk(0)
    key_a(2)
    finish_chunk(1)
    key_b(2)
    finish_chunk(2)
    l_gw.wait()
    l_uw.wait()
    gate_up(0)
    finish_chunk(3)
    gate_up(1)
    gate_up(2)
    far(key_a, 3)
    gate_up(3)
    with scope("act"):
        gate_act = acc[0]
        hidden = (gate_act / (1.0 + jnp.exp(-gate_act)) * acc[1]).astype(BF16)
        l_dw.wait()

    def down(k):
        value = jnp.dot(hidden, dw[:, k * 2 * rw : (k + 1) * 2 * rw], preferred_element_type=F32)
        value = value.astype(BF16)
        for c in (2 * k, 2 * k + 1):
            start = (c % 2) * rw
            part[c] = value[:, start : start + rw].reshape(2, 2, 2, slots, rw)
            send(part.at[c, :, 1 - bc], r1.at[c], 2, rrecv.at[0, k], nc)

    def sum_cores(k):
        with scope("sc%d" % k):
            received(r1.at[pl.ds(0, 2)], rrecv.at[0, k])
            for c in (2 * k, 2 * k + 1):
                for a in range(2):
                    for b in range(2):
                        s1[c, a, b] = (part[c, a, bc, b].astype(F32) + r1[c, a, b].astype(F32)).astype(BF16)
            send(s1.at[2 * k, :, 1 - bx], r2.at[2 * k], 3, rrecv.at[1, k], nx)
            send(s1.at[2 * k + 1, 1 - by], r2.at[2 * k + 1], 3, rrecv.at[1, k], ny)

    def sum_first(k):
        with scope("sf%d" % k):
            received(r2.at[pl.ds(0, 2)], rrecv.at[1, k])
            for c in (2 * k, 2 * k + 1):
                for a in range(2):
                    mine = s1[c, a, bx] if c % 2 == 0 else s1[c, by, a]
                    s2[c, a] = (mine.astype(F32) + r2[c, a].astype(F32)).astype(BF16)
            send(s2.at[2 * k, 1 - by], r3.at[2 * k], 4, rrecv.at[2, k], ny)
            send(s2.at[2 * k + 1, 1 - bx], r3.at[2 * k + 1], 4, rrecv.at[2, k], nx)

    def sum_second(k):
        with scope("ss%d" % k):
            received(r3.at[pl.ds(0, 2)], rrecv.at[2, k])
            for c in (2 * k, 2 * k + 1):
                keep = by if c % 2 == 0 else bx
                total = s2[c, keep].astype(F32) + r3[c].astype(F32)
                for e in range(groups):
                    rbuf[c, e] = total[e * CAP : (e + 1) * CAP].astype(BF16)
                for o in others:
                    send(rbuf.at[c, o], res_hbm.at[c, g], 5, brecv.at[0], dev(o, m))
                store(rbuf.at[c, g], res_hbm.at[c, g], 1)

    with scope("down"):
        for k in range(RCHUNKS // 2):
            down(k)
    sum_cores(0)
    sum_cores(1)
    far(key_b, 3)
    with scope("vuw"):
        l_vu.wait()
    far(key_w, 0)
    attend(0, 1)
    sum_first(0)
    sum_cores(2)
    attend(1, 2)
    sum_first(1)
    sum_cores(3)
    sum_second(0)
    attend(2, 3)
    sum_first(2)
    sum_second(1)
    attend(3, 4)
    sum_first(3)
    sum_second(2)
    attend(4, 5)
    sum_second(3)
    attend(5, 8)

    with scope("z_res"):
        received(res_hbm.at[:, pl.ds(0, groups - 1)], brecv.at[0])
    with scope("z_sends"):
        sources = [
            outg.at[:, pl.ds(0, groups - 1)],
            arr.at[:, pl.ds(0, 7)],
            r1,
            r2,
            r3,
            rbuf.at[:, pl.ds(0, groups - 1)],
        ]
        for kind, source in enumerate(sources):
            rcopy(source, source, send_sem.at[kind], brecv.at[0], nx).wait_send()
        for s in range(groups):
            def sent_keys(like, way):
                rcopy(like, like, ksend.at[way, s], krecv.at[way, s], nx).wait_send()

            if s == 0:
                sent_keys(kwhole(0), 1)
            if s < top_plane:
                @pl.when((g >= s) & (g < top_plane))
                def _():
                    sent_keys(kwhole(0), 0)
                    sent_keys(kwhole(0), 2)

            @functools.partial(guarded, s)
            def _():
                sent_keys(keys.at[pl.ds(0, 2), :, pl.ds(0, sent)], 3)

        pltpu.make_async_copy(wmix, wmix_hbm, store_sem.at[0]).wait()
        pltpu.make_async_copy(rbuf.at[:, 0], res_hbm.at[:, 0], store_sem.at[1]).wait()
        pltpu.make_async_copy(att_ref, att_hbm, store_sem.at[2]).wait()


def finish(res_hbm, wmix_hbm, att_hbm, rout_hbm, out_hbm, res, wmix, att, rout, sem):
    chunks, groups, _, cw = res.shape
    step = chunks // PIECES
    w_load = pltpu.make_async_copy(wmix_hbm, wmix, sem.at[0])
    w_load.start()
    loads = []
    for p in range(PIECES):
        piece = pl.ds(p * step, step)
        loads.append(pltpu.make_async_copy(res_hbm.at[piece], res.at[piece], sem.at[1 + p]))
        loads[p].start()
    a_load = pltpu.make_async_copy(att_hbm, att, sem.at[1 + PIECES])
    a_load.start()
    w_load.wait()
    stores = []
    for p in range(PIECES):
        loads[p].wait()
        for c in range(p * step, (p + 1) * step):
            blocks = [res[c, e].astype(F32) for e in range(groups)]
            block_rows = jnp.concatenate(blocks, axis=0).astype(BF16)
            tall = jnp.concatenate([block_rows] * 3, axis=0)
            rout[:, c * cw : (c + 1) * cw] = jnp.dot(
                wmix[:, : tall.shape[0]], tall, preferred_element_type=F32
            ).astype(BF16)
        cols = pl.ds(p * step * cw, step * cw)
        stores.append(
            pltpu.make_async_copy(rout.at[:, cols], rout_hbm.at[:, cols], sem.at[2 + PIECES + p])
        )
        stores[p].start()
    a_load.wait()
    stores.append(pltpu.make_async_copy(att, out_hbm, sem.at[2 + 2 * PIECES]))
    stores[-1].start()
    for cp in stores:
        cp.wait()


def local(n_ctx, n_sec, qn, qr, klat, krope, ku, vu, tok, ids, gates, gw, uw, dw):
    devices = n_ctx * n_sec
    groups = devices // SPLIT
    slots = groups * CAP
    rows = qn.shape[0]
    heads, lat, nope = ku.shape
    ropew = krope.shape[1]
    tokens, width = tok.shape
    cw = width // CHUNKS
    rw = width // RCHUNKS
    kw = lat + 2 * ropew + 128
    hb = 4 if n_ctx * rows <= 2048 else 1
    lanes = -(-3 * slots // 128) * 128
    dims = (groups, n_sec, rows, heads, lat, ropew, nope, hb)
    a = pl.BlockSpec(memory_space=pl.ANY)
    dma = pltpu.SemaphoreType.DMA
    out_width = heads * vu.shape[2]
    att, res, wmix = pl.pallas_call(
        functools.partial(kernel, dims),
        out_shape=(
            jax.ShapeDtypeStruct((rows, out_width), BF16),
            jax.ShapeDtypeStruct((RCHUNKS, groups, CAP, rw), BF16),
            jax.ShapeDtypeStruct((tokens, lanes), BF16),
        ),
        in_specs=[a] * 12,
        out_specs=(a, a, a),
        scratch_shapes=[
            pltpu.VMEM(ids.shape[::-1], ids.dtype),
            pltpu.VMEM(gates.shape[::-1], gates.dtype),
            pltpu.VMEM(krope.shape, BF16),
            pltpu.VMEM((tokens, lanes), BF16),
            pltpu.VMEM((rows, out_width), BF16),
            pltpu.VMEM(tok.shape, BF16),
            pltpu.VMEM(qn.shape, BF16),
            pltpu.VMEM(qr.shape, BF16),
            pltpu.VMEM(ku.shape, BF16),
            pltpu.VMEM(vu.shape, BF16),
            pltpu.VMEM(gw.shape, BF16),
            pltpu.VMEM(uw.shape, BF16),
            pltpu.VMEM(dw.shape, BF16),
            pltpu.VMEM((heads * rows, kw), BF16),
            pltpu.VMEM((n_ctx, rows, kw), BF16),
            pltpu.VMEM((CHUNKS, groups, CAP, cw), BF16),
            pltpu.VMEM((CHUNKS, groups, CAP, cw), BF16),
            pltpu.VMEM((CHUNKS, SPLIT, slots, cw), BF16),
            pltpu.VMEM((2, SPLIT * slots, gw.shape[1]), F32),
            pltpu.VMEM((RCHUNKS, 2, 2, 2, slots, rw), BF16),
            pltpu.VMEM((RCHUNKS, 2, 2, slots, rw), BF16),
            pltpu.VMEM((RCHUNKS, 2, 2, slots, rw), BF16),
            pltpu.VMEM((RCHUNKS, 2, slots, rw), BF16),
            pltpu.VMEM((RCHUNKS, 2, slots, rw), BF16),
            pltpu.VMEM((RCHUNKS, slots, rw), BF16),
            pltpu.VMEM((RCHUNKS, groups, CAP, rw), BF16),
            dma((11 + CHUNKS,)),
            dma((3,)),
            dma((6,)),
            dma((4, groups)),
            dma((4, groups)),
            dma((CHUNKS,)),
            dma((CHUNKS, 4)),
            dma((3, RCHUNKS // 2)),
            dma((1,)),
        ],
        compiler_params=pltpu.CompilerParams(
            collective_id=0, has_side_effects=True, vmem_limit_bytes=67043328
        ),
    )(ids.T, gates.T, klat, krope, tok, qn, qr, ku, vu, gw, uw, dw)
    rout, att = pl.pallas_call(
        finish,
        out_shape=(jax.ShapeDtypeStruct(tok.shape, BF16), jax.ShapeDtypeStruct(att.shape, BF16)),
        in_specs=[a, a, a],
        out_specs=(a, a),
        scratch_shapes=[
            pltpu.VMEM(res.shape, BF16),
            pltpu.VMEM(wmix.shape, BF16),
            pltpu.VMEM(att.shape, BF16),
            pltpu.VMEM(tok.shape, BF16),
            dma((3 + 2 * PIECES,)),
        ],
    )(res, wmix, att)
    return att, rout


def solution(mesh):
    body = functools.partial(local, mesh.shape["ctx"], mesh.shape["sec"])
    both = ("ctx", "sec")
    return jax.shard_map(
        body,
        mesh=mesh,
        in_specs=(
            P("ctx", "sec"),
            P("ctx", "sec"),
            P("ctx", None),
            P("ctx", None),
            P("sec", None, None),
            P("sec", None, None),
            P(both, None),
            P(both, None),
            P(both, None),
            P(None, both),
            P(None, both),
            P(both, None),
        ),
        out_specs=(P("ctx", "sec"), P(both, None)),
        check_vma=False,
    )
```

```python
import functools

import jax
import jax.numpy as jnp
from jax import lax
from jax.experimental import pallas as pl
from jax.experimental.pallas import tpu as pltpu
from jax.sharding import PartitionSpec as P

CAP = 4
SPLIT = 8
CHUNKS = 4
RCHUNKS = 8
PIECES = 2
LOG2E = 1.4426950408889634
MESH_ID = pl.DeviceIdType.MESH
F32 = jnp.float32
BF16 = jnp.bfloat16
NT = (((1,), (1,)), ((), ()))
scope = jax.named_scope


def kernel(
    dims,
    ids_hbm,
    gates_hbm,
    klat_hbm,
    krope_hbm,
    tok_hbm,
    qn_hbm,
    qr_hbm,
    ku_hbm,
    vu_hbm,
    gw_hbm,
    uw_hbm,
    dw_hbm,
    att_hbm,
    res_hbm,
    wmix_hbm,
    ids_ref,
    gates_ref,
    krope_ref,
    wmix,
    att_ref,
    tok,
    qn,
    qr,
    ku,
    vu,
    gw,
    uw,
    dw,
    qcat,
    keys,
    outg,
    zbuf,
    arr,
    acc,
    part,
    r1,
    s1,
    r2,
    s2,
    r3,
    rbuf,
    load_sem,
    store_sem,
    send_sem,
    ksend,
    krecv,
    zrecv,
    arecv,
    rrecv,
    brecv,
):
    groups, n_sec, rows, heads, lat, ropew, nope, hb = dims
    slots = groups * CAP
    width = tok.shape[1]
    cw = width // CHUNKS
    rw = width // RCHUNKS
    tokens = tok.shape[0]
    sent = lat + 2 * ropew
    ctx = lax.axis_index("ctx")
    sec = lax.axis_index("sec")
    me = ctx * n_sec + sec
    g = me // SPLIT
    m = lax.rem(me, SPLIT)
    bx = lax.rem(m, 2)
    bc = lax.rem(m // 2, 2)
    by = m // 4
    mx = m + 1 - 2 * bx
    mc = m + 2 - 4 * bc
    my = m + 4 - 8 * by
    mxy = mx + my - m

    def dev(group, member):
        index = group * SPLIT + member
        return (index // n_sec, lax.rem(index, n_sec))


    def rcopy(src, dst, ss, rs, target):
        return pltpu.make_async_remote_copy(
            src_ref=src, dst_ref=dst, send_sem=ss, recv_sem=rs,
            device_id=target, device_id_type=MESH_ID,
        )

    def send(src, dst, kind, rs, target):
        rcopy(src, dst, send_sem.at[kind], rs, target).start()

    def received(like, rs):
        rcopy(like, like, send_sem.at[0], rs, nx).wait_recv()

    def store(src, dst, kind):
        pltpu.make_async_copy(src, dst, store_sem.at[kind]).start()

    nx, nc, ny = dev(g, mx), dev(g, mc), dev(g, my)
    others = [lax.rem(g + step, groups) for step in range(1, groups)]
    every = [g] + others

    barrier = pltpu.get_barrier_semaphore()
    for target in [dev(o, m) for o in others] + [nx, nc, ny]:
        pl.semaphore_signal(barrier, inc=1, device_id=target, device_id_type=MESH_ID)

    own_keys = keys.at[ctx]
    pairs = [
        (ids_hbm, ids_ref), (gates_hbm, gates_ref), (qn_hbm, qn), (qr_hbm, qr), (ku_hbm, ku),
        (gw_hbm, gw), (uw_hbm, uw), (dw_hbm, dw), (vu_hbm, vu),
        (klat_hbm, own_keys.at[:, pl.ds(0, lat)]), (krope_hbm, krope_ref),
    ]
    loads = [pltpu.make_async_copy(a, b, load_sem.at[i]) for i, (a, b) in enumerate(pairs)]
    l_ids, l_gates, l_qn, l_qr, l_ku, l_gw, l_uw, l_dw, l_vu, l_klat, l_krope = loads
    l_ids.start()
    l_gates.start()
    tok_loads = []
    for c in range(CHUNKS):
        cols = pl.ds(c * cw, cw)
        tok_loads.append(
            pltpu.make_async_copy(
                tok_hbm.at[:, cols], tok.at[:, cols], load_sem.at[len(loads) + c]
            )
        )
        tok_loads[c].start()
    l_klat.start()
    l_krope.start()

    def kwhole(shard):
        return keys.at[shard, :, pl.ds(0, sent)]

    def kshard(group, member):
        return (group * SPLIT + member) // n_sec

    def kslot(way, s):
        return (groups + 1, groups, 2 * groups + 1, 0)[way] + s

    def whole(group, member, way, s, target, rs=None):
        piece = kwhole(kshard(group, member))
        rcopy(piece, piece, ksend.at[kslot(way, s)], krecv.at[kslot(way, s if rs is None else rs)], target).start()

    up = dev(lax.rem(g + 1, groups), m)
    top_plane = groups - 1

    def guarded(s, fn):
        if s == 0:
            fn()
        else:
            pl.when(g >= s)(fn)

    def key_up(s, member, way):
        if s >= top_plane:
            return
        cond = g < top_plane if s == 0 else (g >= s) & (g < top_plane)

        @pl.when(cond)
        def _():
            whole(g - s, member, way, s, up, s + 1)

    def key_own():
        whole(g, m, 1, 0, ny)
        whole(g, m, 3, 0, nc)

    def key_pass(s, member, way):
        with scope("kp%d_%d" % (s, way)):
            if s == 0 and way == 0:
                key_up(0, m, 0)
                return

            @functools.partial(guarded, s)
            def _():
                received(kwhole(0), krecv.at[kslot(1 if s == 0 else way, s)])

            key_up(s, member, way)

            @functools.partial(guarded, s)
            def _():
                whole(g - s, member, 3, s, nc)

    def key_a(s):
        key_pass(s, m, 0)

    def key_b(s):
        key_pass(s, my, 2)

    def key_w(s):
        with scope("kw%d" % s):
            @functools.partial(guarded, s)
            def _():
                received(keys.at[pl.ds(0, 2), :, pl.ds(0, sent)], krecv.at[kslot(3, s)])

    with scope("a_sel"):
        lanes = wmix.shape[1]
        row = lax.broadcasted_iota(jnp.int32, (lanes, tokens), 0)
        slot = row & (slots - 1)
        expert = slot // CAP
        matches = jnp.zeros((lanes, tokens), F32)
        gate = jnp.zeros((lanes, tokens), F32)
        l_ids.wait()
        l_gates.wait()
        for load in (l_qn, l_qr, l_ku):
            load.start()
        for k in range(ids_ref.shape[0]):
            hit = ids_ref[k : k + 1, :] == expert
            matches = jnp.where(hit, 1.0, matches)
            gate = gate + jnp.where(hit, gates_ref[k : k + 1, :], 0.0)
        earlier = (
            lax.broadcasted_iota(jnp.int32, (tokens, tokens), 0)
            < lax.broadcasted_iota(jnp.int32, (tokens, tokens), 1)
        )
        rank = jnp.dot(
            matches.astype(BF16), jnp.where(earlier, 1.0, 0.0).astype(BF16), preferred_element_type=F32
        )
        chosen = jnp.where(rank == (slot & (CAP - 1)).astype(F32), matches, 0.0)
        picker = chosen[:slots].astype(BF16)

    with scope("b_pick"):
        for c in range(CHUNKS):
            tok_loads[c].wait()
            picked = jnp.dot(picker, tok[:, c * cw : (c + 1) * cw], preferred_element_type=F32)
            for e in range(groups):
                outg[c, e] = picked[e * CAP : (e + 1) * CAP].astype(BF16)
        l_klat.wait()
        l_krope.wait()
        own_keys[:, lat:sent] = jnp.concatenate([krope_ref[...], krope_ref[...]], axis=1)

    with scope("c_barrier"):
        pl.semaphore_wait(barrier, 3 + len(others))

    with scope("d_zsend"):
        for c in range(CHUNKS):
            for i, o in enumerate(others):
                send(outg.at[c, o], zbuf.at[c, g], 0, zrecv.at[c], dev(o, m))
        key_own()

    with scope("e_wmix"):
        weight = chosen * gate
        w1 = weight.astype(BF16).astype(F32)
        w2 = (weight - w1).astype(BF16).astype(F32)
        w3 = weight - w1 - w2
        wmix[...] = jnp.where(
            row < slots, w1, jnp.where(row < 2 * slots, w2, jnp.where(row < 3 * slots, w3, 0.0))
        ).T.astype(BF16)
        store(wmix, wmix_hbm, 0)

        maskw = keys.shape[2] - sent

        @pl.loop(0, keys.shape[0])
        def _(shard):
            key_place = shard * rows + lax.broadcasted_iota(jnp.int32, (rows, maskw), 0)
            query = lax.broadcasted_iota(jnp.int32, (rows, maskw), 1)
            hidden_key = (key_place > ctx * rows + query) & (query < rows)
            keys[shard, :, sent:] = jnp.where(hidden_key, -1e30, 0.0).astype(BF16)

        unit = jnp.where(
            lax.broadcasted_iota(jnp.int32, (rows, maskw), 0)
            == lax.broadcasted_iota(jnp.int32, (rows, maskw), 1),
            1.0,
            0.0,
        ).astype(BF16)

    per = SPLIT // n_sec
    with scope("zero"):
        for s in range(1, groups):
            @pl.when(g + s < groups)
            def _():
                keys[pl.ds((g + s) * per, per), :, :sent] = jnp.zeros((per, rows, sent), BF16)

    with scope("f_loads"):
        l_qn.wait()
        l_qr.wait()
        l_ku.wait()
        for load in (l_gw, l_uw, l_dw, l_vu):
            load.start()

    def query_latents(first, last):
        with scope("ql"):
            @pl.loop(first, last)
            def _(p):
                rope = qr[:, pl.ds(pl.multiple_of(p * 2 * ropew, 2 * ropew), 2 * ropew)]
                low = lax.broadcasted_iota(jnp.int32, rope.shape, 1) < ropew
                for k in range(2):
                    h = p * 2 + k
                    q = qn[:, pl.ds(pl.multiple_of(h * nope, nope), nope)]
                    latent = lax.dot_general(q, ku[h], NT, preferred_element_type=F32)
                    place = pl.ds(pl.multiple_of(h * rows, rows), rows)
                    qcat[place, :lat] = latent.astype(BF16)
                    keep = low if k == 0 else jnp.logical_not(low)
                    qcat[place, lat:sent] = jnp.where(keep, rope.astype(F32), 0.0).astype(BF16)
                    qcat[place, sent:] = unit

    def spread(member, c, way, target):
        piece = arr.at[c, member]
        send(piece, piece, 1, arecv.at[c, way], target)

    def arrive(c, way):
        received(arr.at[c, 0] if way < 3 else arr.at[c, pl.ds(0, 4)], arecv.at[c, way])

    def start_chunk(c):
        with scope("s%d" % c):
            received(zbuf.at[c, pl.ds(0, groups - 1)], zrecv.at[c])
            zbuf[c, g] = outg[c, g]
            blocks = [zbuf[c, e].astype(F32) for e in range(groups)]
            arr[c, m] = jnp.concatenate(blocks, axis=0).astype(BF16)
            spread(m, c, 0, nx)
            spread(m, c, 1, ny)
            spread(m, c, 3, nc)

    def forward_chunk(c):
        with scope("fw%d" % c):
            arrive(c, 0)
            if c % 2 == 0:
                spread(mx, c, 2, ny)
            spread(mx, c, 3, nc)
            arrive(c, 1)
            if c % 2 == 1:
                spread(my, c, 2, nx)
            spread(my, c, 3, nc)

    count = SPLIT * slots

    def finish_chunk(c):
        with scope("fin%d" % c):
            arrive(c, 2)
            spread(mxy, c, 3, nc)

    def gate_up(c):
        with scope("guw%d" % c):
            arrive(c, 3)
        with scope("gu%d" % c):
            x = arr[c].reshape(count, cw)
            g_part = jnp.dot(x, gw[c * cw : (c + 1) * cw], preferred_element_type=F32)
            u_part = jnp.dot(x, uw[c * cw : (c + 1) * cw], preferred_element_type=F32)
            if c == 0:
                acc[0] = g_part
                acc[1] = u_part
            else:
                acc[0] += g_part
                acc[1] += u_part

    pairs_n = heads // 2

    def ql(a, b):
        query_latents(a * pairs_n // 8, b * pairs_n // 8)

    seq = keys.shape[0] * keys.shape[1]
    scale = (nope + ropew) ** -0.5 * LOG2E
    vdim = vu.shape[2]

    def attend(first, last, most):
        size = min(hb, most)
        block = size * rows
        with scope("att%d" % first):
            @pl.loop(first // size, last // size)
            def _(b):
                q = qcat[pl.ds(pl.multiple_of(b * block, block), block)]
                kk = keys[...].reshape(seq, keys.shape[2])
                score = lax.dot_general(q, kk, NT, preferred_element_type=F32)
                top = jnp.max(score, axis=1, keepdims=True)
                expo = jnp.exp2((score - top) * scale)
                total = jnp.sum(expo, axis=1, keepdims=True)
                mixed = jnp.dot(expo.astype(BF16), kk[:, :lat], preferred_element_type=F32)
                mixed = (mixed / total).astype(BF16)
                for k in range(size):
                    h = b * size + k
                    value = jnp.dot(
                        mixed[k * rows : (k + 1) * rows], vu[h], preferred_element_type=F32
                    )
                    att_ref[:, pl.ds(pl.multiple_of(h * vdim, vdim), vdim)] = value.astype(BF16)

            cols = pl.ds(first * vdim, (last - first) * vdim)
            store(att_ref.at[:, cols], att_hbm.at[:, cols], 2)

    def far(fn, first):
        for s in range(first, groups):
            fn(s)

    ql(0, 4)
    start_chunk(0)
    key_a(0)
    start_chunk(1)
    key_b(0)
    ql(4, 5)
    start_chunk(2)
    ql(5, 6)
    start_chunk(3)
    forward_chunk(0)
    ql(6, 7)
    key_a(1)
    forward_chunk(1)
    ql(7, 8)
    forward_chunk(2)
    key_b(1)
    forward_chunk(3)
    finish_chunk(0)
    finish_chunk(1)
    key_a(2)
    finish_chunk(2)
    l_gw.wait()
    l_uw.wait()
    gate_up(0)
    key_b(2)
    finish_chunk(3)
    gate_up(1)
    gate_up(2)
    gate_up(3)
    with scope("act"):
        gate_act = acc[0]
        hidden = (gate_act / (1.0 + jnp.exp(-gate_act)) * acc[1]).astype(BF16)
        l_dw.wait()

    def down(k):
        value = jnp.dot(hidden, dw[:, k * 2 * rw : (k + 1) * 2 * rw], preferred_element_type=F32)
        value = value.astype(BF16)
        for c in (2 * k, 2 * k + 1):
            start = (c % 2) * rw
            part[c] = value[:, start : start + rw].reshape(2, 2, 2, slots, rw)
            send(part.at[c, :, 1 - bc], r1.at[c], 2, rrecv.at[0, k], nc)

    def sum_cores(k):
        with scope("sc%d" % k):
            received(r1.at[pl.ds(0, 2)], rrecv.at[0, k])
            for c in (2 * k, 2 * k + 1):
                for a in range(2):
                    for b in range(2):
                        s1[c, a, b] = (part[c, a, bc, b].astype(F32) + r1[c, a, b].astype(F32)).astype(BF16)
            send(s1.at[2 * k, :, 1 - bx], r2.at[2 * k], 3, rrecv.at[1, k], nx)
            send(s1.at[2 * k + 1, 1 - by], r2.at[2 * k + 1], 3, rrecv.at[1, k], ny)

    def sum_first(k):
        with scope("sf%d" % k):
            received(r2.at[pl.ds(0, 2)], rrecv.at[1, k])
            for c in (2 * k, 2 * k + 1):
                for a in range(2):
                    mine = s1[c, a, bx] if c % 2 == 0 else s1[c, by, a]
                    s2[c, a] = (mine.astype(F32) + r2[c, a].astype(F32)).astype(BF16)
            send(s2.at[2 * k, 1 - by], r3.at[2 * k], 4, rrecv.at[2, k], ny)
            send(s2.at[2 * k + 1, 1 - bx], r3.at[2 * k + 1], 4, rrecv.at[2, k], nx)

    def sum_second(k):
        with scope("ss%d" % k):
            received(r3.at[pl.ds(0, 2)], rrecv.at[2, k])
            for c in (2 * k, 2 * k + 1):
                keep = by if c % 2 == 0 else bx
                total = s2[c, keep].astype(F32) + r3[c].astype(F32)
                for e in range(groups):
                    rbuf[c, e] = total[e * CAP : (e + 1) * CAP].astype(BF16)
                for o in others:
                    send(rbuf.at[c, o], res_hbm.at[c, g], 5, brecv.at[0], dev(o, m))
                store(rbuf.at[c, g], res_hbm.at[c, g], 1)

    with scope("down"):
        for k in range(RCHUNKS // 2):
            down(k)
    far(key_a, 3)
    sum_cores(0)
    sum_cores(1)
    far(key_b, 3)
    with scope("vuw"):
        l_vu.wait()
    far(key_w, 0)
    attend(heads * 0 // 32, heads * 4 // 32, 4)
    sum_first(0)
    sum_cores(2)
    sum_first(1)
    sum_cores(3)
    attend(heads * 4 // 32, heads * 8 // 32, 4)
    sum_second(0)
    sum_first(2)
    attend(heads * 8 // 32, heads * 12 // 32, 4)
    sum_second(1)
    sum_first(3)
    attend(heads * 12 // 32, heads * 16 // 32, 4)
    sum_second(2)
    sum_second(3)
    attend(heads * 16 // 32, heads * 32 // 32, 16)

    with scope("z_res"):
        received(res_hbm.at[:, pl.ds(0, groups - 1)], brecv.at[0])
    with scope("z_sends"):
        sources = [
            outg.at[:, pl.ds(0, groups - 1)],
            arr.at[:, pl.ds(0, 7)],
            r1,
            r2,
            r3,
            rbuf.at[:, pl.ds(0, groups - 1)],
        ]
        for kind, source in enumerate(sources):
            rcopy(source, source, send_sem.at[kind], brecv.at[0], nx).wait_send()
        for s in range(groups):
            def sent_keys(like, way):
                rcopy(like, like, ksend.at[kslot(way, s)], krecv.at[0], nx).wait_send()

            if s == 0:
                sent_keys(kwhole(0), 1)
            if s < top_plane:
                @pl.when((g >= s) & (g < top_plane))
                def _():
                    sent_keys(kwhole(0), 0)
                    sent_keys(kwhole(0), 2)

            @functools.partial(guarded, s)
            def _():
                sent_keys(keys.at[pl.ds(0, 2), :, pl.ds(0, sent)], 3)

        pltpu.make_async_copy(wmix, wmix_hbm, store_sem.at[0]).wait()
        pltpu.make_async_copy(rbuf.at[:, 0], res_hbm.at[:, 0], store_sem.at[1]).wait()
        pltpu.make_async_copy(att_ref, att_hbm, store_sem.at[2]).wait()


def finish(res_hbm, wmix_hbm, att_hbm, rout_hbm, out_hbm, res, wmix, att, rout, sem):
    chunks, groups, _, cw = res.shape
    step = chunks // PIECES
    w_load = pltpu.make_async_copy(wmix_hbm, wmix, sem.at[0])
    w_load.start()
    loads = []
    for p in range(PIECES):
        piece = pl.ds(p * step, step)
        loads.append(pltpu.make_async_copy(res_hbm.at[piece], res.at[piece], sem.at[1 + p]))
        loads[p].start()
    a_load = pltpu.make_async_copy(att_hbm, att, sem.at[1 + PIECES])
    a_load.start()
    with scope("fw"):
        w_load.wait()
    stores = []
    for p in range(PIECES):
        with scope("fl%d" % p):
            loads[p].wait()
        for c in range(p * step, (p + 1) * step):
            blocks = [res[c, e].astype(F32) for e in range(groups)]
            block_rows = jnp.concatenate(blocks, axis=0).astype(BF16)
            tall = jnp.concatenate([block_rows] * 3, axis=0)
            rout[:, c * cw : (c + 1) * cw] = jnp.dot(
                wmix[:, : tall.shape[0]], tall, preferred_element_type=F32
            ).astype(BF16)
        cols = pl.ds(p * step * cw, step * cw)
        stores.append(
            pltpu.make_async_copy(rout.at[:, cols], rout_hbm.at[:, cols], sem.at[2 + PIECES + p])
        )
        stores[p].start()
        if p == 0:
            a_load.wait()
            a_store = pltpu.make_async_copy(att, out_hbm, sem.at[2 + 2 * PIECES])
            a_store.start()
    with scope("fz"):
        for cp in stores + [a_store]:
            cp.wait()


def local(n_ctx, n_sec, qn, qr, klat, krope, ku, vu, tok, ids, gates, gw, uw, dw):
    devices = n_ctx * n_sec
    groups = devices // SPLIT
    slots = groups * CAP
    rows = qn.shape[0]
    heads, lat, nope = ku.shape
    ropew = krope.shape[1]
    tokens, width = tok.shape
    cw = width // CHUNKS
    rw = width // RCHUNKS
    kw = lat + 2 * ropew + 128
    hb = 16 if n_ctx * rows <= 2048 else 1
    lanes = -(-3 * slots // 128) * 128
    dims = (groups, n_sec, rows, heads, lat, ropew, nope, hb)
    a = pl.BlockSpec(memory_space=pl.ANY)
    dma = pltpu.SemaphoreType.DMA
    out_width = heads * vu.shape[2]
    att, res, wmix = pl.pallas_call(
        functools.partial(kernel, dims),
        out_shape=(
            jax.ShapeDtypeStruct((rows, out_width), BF16),
            jax.ShapeDtypeStruct((RCHUNKS, groups, CAP, rw), BF16),
            jax.ShapeDtypeStruct((tokens, lanes), BF16),
        ),
        in_specs=[a] * 12,
        out_specs=(a, a, a),
        scratch_shapes=[
            pltpu.VMEM(ids.shape[::-1], ids.dtype),
            pltpu.VMEM(gates.shape[::-1], gates.dtype),
            pltpu.VMEM(krope.shape, BF16),
            pltpu.VMEM((tokens, lanes), BF16),
            pltpu.VMEM((rows, out_width), BF16),
            pltpu.VMEM(tok.shape, BF16),
            pltpu.VMEM(qn.shape, BF16),
            pltpu.VMEM(qr.shape, BF16),
            pltpu.VMEM(ku.shape, BF16),
            pltpu.VMEM(vu.shape, BF16),
            pltpu.VMEM(gw.shape, BF16),
            pltpu.VMEM(uw.shape, BF16),
            pltpu.VMEM(dw.shape, BF16),
            pltpu.VMEM((heads * rows, kw), BF16),
            pltpu.VMEM((n_ctx, rows, kw), BF16),
            pltpu.VMEM((CHUNKS, groups, CAP, cw), BF16),
            pltpu.VMEM((CHUNKS, groups, CAP, cw), BF16),
            pltpu.VMEM((CHUNKS, SPLIT, slots, cw), BF16),
            pltpu.VMEM((2, SPLIT * slots, gw.shape[1]), F32),
            pltpu.VMEM((RCHUNKS, 2, 2, 2, slots, rw), BF16),
            pltpu.VMEM((RCHUNKS, 2, 2, slots, rw), BF16),
            pltpu.VMEM((RCHUNKS, 2, 2, slots, rw), BF16),
            pltpu.VMEM((RCHUNKS, 2, slots, rw), BF16),
            pltpu.VMEM((RCHUNKS, 2, slots, rw), BF16),
            pltpu.VMEM((RCHUNKS, slots, rw), BF16),
            pltpu.VMEM((RCHUNKS, groups, CAP, rw), BF16),
            dma((11 + CHUNKS,)),
            dma((3,)),
            dma((6,)),
            dma((3 * groups + 1,)),
            dma((3 * groups + 1,)),
            dma((CHUNKS,)),
            dma((CHUNKS, 4)),
            dma((3, RCHUNKS // 2)),
            dma((1,)),
        ],
        compiler_params=pltpu.CompilerParams(
            collective_id=0, has_side_effects=True, vmem_limit_bytes=67043328
        ),
    )(ids.T, gates.T, klat, krope, tok, qn, qr, ku, vu, gw, uw, dw)
    rout, att = pl.pallas_call(
        finish,
        out_shape=(jax.ShapeDtypeStruct(tok.shape, BF16), jax.ShapeDtypeStruct(att.shape, BF16)),
        in_specs=[a, a, a],
        out_specs=(a, a),
        scratch_shapes=[
            pltpu.VMEM(res.shape, BF16),
            pltpu.VMEM(wmix.shape, BF16),
            pltpu.VMEM(att.shape, BF16),
            pltpu.VMEM(tok.shape, BF16),
            dma((3 + 2 * PIECES,)),
        ],
    )(res, wmix, att)
    return att, rout


def solution(mesh):
    body = functools.partial(local, mesh.shape["ctx"], mesh.shape["sec"])
    both = ("ctx", "sec")
    return jax.shard_map(
        body,
        mesh=mesh,
        in_specs=(
            P("ctx", "sec"),
            P("ctx", "sec"),
            P("ctx", None),
            P("ctx", None),
            P("sec", None, None),
            P("sec", None, None),
            P(both, None),
            P(both, None),
            P(both, None),
            P(None, both),
            P(None, both),
            P(both, None),
        ),
        out_specs=(P("ctx", "sec"), P(both, None)),
        check_vma=False,
    )
```

```python
import functools

import jax
import jax.numpy as jnp
from jax import lax
from jax.experimental import pallas as pl
from jax.experimental.pallas import tpu as pltpu
from jax.sharding import PartitionSpec as P

CAP = 4
SPLIT = 8
CHUNKS = 4
RCHUNKS = 8
PIECES = 2
LOG2E = 1.4426950408889634
MESH_ID = pl.DeviceIdType.MESH
F32 = jnp.float32
BF16 = jnp.bfloat16
NT = (((1,), (1,)), ((), ()))
scope = jax.named_scope


def kernel(
    dims,
    ids_hbm,
    gates_hbm,
    klat_hbm,
    krope_hbm,
    tok_hbm,
    qn_hbm,
    qr_hbm,
    ku_hbm,
    vu_hbm,
    gw_hbm,
    uw_hbm,
    dw_hbm,
    att_hbm,
    res_hbm,
    wmix_hbm,
    ids_ref,
    gates_ref,
    krope_ref,
    wmix,
    att_ref,
    tok,
    qn,
    qr,
    ku,
    vu,
    gw,
    uw,
    dw,
    qcat,
    keys,
    outg,
    own,
    arr,
    acc,
    part,
    r1,
    s1,
    r2,
    s2,
    r3,
    rbuf,
    load_sem,
    store_sem,
    send_sem,
    ksend,
    krecv,
    zrecv,
    orecv,
    arecv,
    rrecv,
    brecv,
):
    groups, n_sec, rows, heads, lat, ropew, nope, hb = dims
    slots = groups * CAP
    width = tok.shape[1]
    cw = width // CHUNKS
    rw = width // RCHUNKS
    tokens = tok.shape[0]
    sent = lat + 2 * ropew
    ctx = lax.axis_index("ctx")
    sec = lax.axis_index("sec")
    me = ctx * n_sec + sec
    g = me // SPLIT
    m = lax.rem(me, SPLIT)
    bx = lax.rem(m, 2)
    bc = lax.rem(m // 2, 2)
    by = m // 4
    mx = m + 1 - 2 * bx
    mc = m + 2 - 4 * bc
    my = m + 4 - 8 * by
    mxy = mx + my - m

    def dev(group, member):
        index = group * SPLIT + member
        return (index // n_sec, lax.rem(index, n_sec))


    def rcopy(src, dst, ss, rs, target):
        return pltpu.make_async_remote_copy(
            src_ref=src, dst_ref=dst, send_sem=ss, recv_sem=rs,
            device_id=target, device_id_type=MESH_ID,
        )

    def send(src, dst, kind, rs, target):
        rcopy(src, dst, send_sem.at[kind], rs, target).start()

    def received(like, rs):
        rcopy(like, like, send_sem.at[0], rs, nx).wait_recv()

    def store(src, dst, kind):
        pltpu.make_async_copy(src, dst, store_sem.at[kind]).start()

    nx, nc, ny = dev(g, mx), dev(g, mc), dev(g, my)
    others = [lax.rem(g + step, groups) for step in range(1, groups)]
    every = [g] + others

    barrier = pltpu.get_barrier_semaphore()
    for target in [dev(o, m) for o in others] + [nx, nc, ny]:
        pl.semaphore_signal(barrier, inc=1, device_id=target, device_id_type=MESH_ID)

    own_keys = keys.at[ctx]
    pairs = [
        (ids_hbm, ids_ref), (gates_hbm, gates_ref), (qn_hbm, qn), (qr_hbm, qr), (ku_hbm, ku),
        (gw_hbm, gw), (uw_hbm, uw), (dw_hbm, dw), (vu_hbm, vu),
        (klat_hbm, own_keys.at[:, pl.ds(0, lat)]), (krope_hbm, krope_ref),
    ]
    loads = [pltpu.make_async_copy(a, b, load_sem.at[i]) for i, (a, b) in enumerate(pairs)]
    l_ids, l_gates, l_qn, l_qr, l_ku, l_gw, l_uw, l_dw, l_vu, l_klat, l_krope = loads
    l_ids.start()
    l_gates.start()
    tok_loads = []
    for c in range(CHUNKS):
        cols = pl.ds(c * cw, cw)
        tok_loads.append(
            pltpu.make_async_copy(
                tok_hbm.at[:, cols], tok.at[:, cols], load_sem.at[len(loads) + c]
            )
        )
        tok_loads[c].start()
    l_klat.start()
    l_krope.start()

    def kwhole(shard):
        return keys.at[shard, :, pl.ds(0, sent)]

    def kshard(group, member):
        return (group * SPLIT + member) // n_sec

    def kslot(way, s):
        return (groups + 1, groups, 2 * groups + 1, 0)[way] + s

    def whole(group, member, way, s, target, rs=None):
        piece = kwhole(kshard(group, member))
        rcopy(piece, piece, ksend.at[kslot(way, s)], krecv.at[kslot(way, s if rs is None else rs)], target).start()

    up = dev(lax.rem(g + 1, groups), m)
    top_plane = groups - 1

    def guarded(s, fn):
        if s == 0:
            fn()
        else:
            pl.when(g >= s)(fn)

    def key_up(s, member, way):
        if s >= top_plane:
            return
        cond = g < top_plane if s == 0 else (g >= s) & (g < top_plane)

        @pl.when(cond)
        def _():
            whole(g - s, member, way, s, up, s + 1)

    def key_own():
        whole(g, m, 1, 0, ny)
        whole(g, m, 3, 0, nc)

    def key_pass(s, member, way):
        with scope("kp%d_%d" % (s, way)):
            if s == 0 and way == 0:
                key_up(0, m, 0)
                return

            @functools.partial(guarded, s)
            def _():
                received(kwhole(0), krecv.at[kslot(1 if s == 0 else way, s)])

            key_up(s, member, way)

            @functools.partial(guarded, s)
            def _():
                whole(g - s, member, 3, s, nc)

    def key_a(s):
        key_pass(s, m, 0)

    def key_b(s):
        key_pass(s, my, 2)

    def key_w(s):
        with scope("kw%d" % s):
            @functools.partial(guarded, s)
            def _():
                received(keys.at[pl.ds(0, 2), :, pl.ds(0, sent)], krecv.at[kslot(3, s)])

    with scope("a_sel"):
        lanes = wmix.shape[1]
        row = lax.broadcasted_iota(jnp.int32, (lanes, tokens), 0)
        slot = row & (slots - 1)
        expert = slot // CAP
        matches = jnp.zeros((lanes, tokens), F32)
        gate = jnp.zeros((lanes, tokens), F32)
        l_ids.wait()
        l_gates.wait()
        for load in (l_qn, l_qr, l_ku):
            load.start()
        for k in range(ids_ref.shape[0]):
            hit = ids_ref[k : k + 1, :] == expert
            matches = jnp.where(hit, 1.0, matches)
            gate = gate + jnp.where(hit, gates_ref[k : k + 1, :], 0.0)
        earlier = (
            lax.broadcasted_iota(jnp.int32, (tokens, tokens), 0)
            < lax.broadcasted_iota(jnp.int32, (tokens, tokens), 1)
        )
        rank = jnp.dot(
            matches.astype(BF16), jnp.where(earlier, 1.0, 0.0).astype(BF16), preferred_element_type=F32
        )
        chosen = jnp.where(rank == (slot & (CAP - 1)).astype(F32), matches, 0.0)
        picker = chosen[:slots].astype(BF16)

    with scope("b_pick"):
        for c in range(CHUNKS):
            tok_loads[c].wait()
            picked = jnp.dot(picker, tok[:, c * cw : (c + 1) * cw], preferred_element_type=F32)
            for e in range(groups):
                outg[c, e] = picked[e * CAP : (e + 1) * CAP].astype(BF16)
        l_klat.wait()
        l_krope.wait()
        own_keys[:, lat:sent] = jnp.concatenate([krope_ref[...], krope_ref[...]], axis=1)

    with scope("c_barrier"):
        pl.semaphore_wait(barrier, 3 + len(others))

    with scope("d_zsend"):
        for c in range(CHUNKS):
            for i, o in enumerate(others):
                send(outg.at[c, o], arr.at[c, m, groups - 2 - i], 0, zrecv.at[c], dev(o, m))
        own[m] = outg[:, g]
        for way, target in enumerate((nx, ny)):
            send(own.at[m], own.at[m], 6, orecv.at[way], target)
        send(own.at[m], own.at[m], 6, orecv.at[3], nc)
        key_own()

    with scope("e_wmix"):
        weight = chosen * gate
        w1 = weight.astype(BF16).astype(F32)
        w2 = (weight - w1).astype(BF16).astype(F32)
        w3 = weight - w1 - w2
        wmix[...] = jnp.where(
            row < slots, w1, jnp.where(row < 2 * slots, w2, jnp.where(row < 3 * slots, w3, 0.0))
        ).T.astype(BF16)
        store(wmix, wmix_hbm, 0)

        maskw = keys.shape[2] - sent

        @pl.loop(0, keys.shape[0])
        def _(shard):
            key_place = shard * rows + lax.broadcasted_iota(jnp.int32, (rows, maskw), 0)
            query = lax.broadcasted_iota(jnp.int32, (rows, maskw), 1)
            hidden_key = (key_place > ctx * rows + query) & (query < rows)
            keys[shard, :, sent:] = jnp.where(hidden_key, -1e30, 0.0).astype(BF16)

        unit = jnp.where(
            lax.broadcasted_iota(jnp.int32, (rows, maskw), 0)
            == lax.broadcasted_iota(jnp.int32, (rows, maskw), 1),
            1.0,
            0.0,
        ).astype(BF16)

    per = SPLIT // n_sec
    with scope("zero"):
        for s in range(1, groups):
            @pl.when(g + s < groups)
            def _():
                keys[pl.ds((g + s) * per, per), :, :sent] = jnp.zeros((per, rows, sent), BF16)

    with scope("f_loads"):
        l_qn.wait()
        l_qr.wait()
        l_ku.wait()
        for load in (l_gw, l_uw, l_dw, l_vu):
            load.start()

    def query_latents(first, last):
        with scope("ql"):
            @pl.loop(first, last)
            def _(p):
                rope = qr[:, pl.ds(pl.multiple_of(p * 2 * ropew, 2 * ropew), 2 * ropew)]
                low = lax.broadcasted_iota(jnp.int32, rope.shape, 1) < ropew
                for k in range(2):
                    h = p * 2 + k
                    q = qn[:, pl.ds(pl.multiple_of(h * nope, nope), nope)]
                    latent = lax.dot_general(q, ku[h], NT, preferred_element_type=F32)
                    place = pl.ds(pl.multiple_of(h * rows, rows), rows)
                    qcat[place, :lat] = latent.astype(BF16)
                    keep = low if k == 0 else jnp.logical_not(low)
                    qcat[place, lat:sent] = jnp.where(keep, rope.astype(F32), 0.0).astype(BF16)
                    qcat[place, sent:] = unit

    def spread(member, c, way, target):
        piece = arr.at[c, member]
        send(piece, piece, 1, arecv.at[c, way], target)

    def arrive(c, way):
        received(arr.at[c, 0] if way < 3 else arr.at[c, pl.ds(0, 4)], arecv.at[c, way])

    def start_chunk(c):
        with scope("s%d" % c):
            received(arr.at[c, 0], zrecv.at[c])
            spread(m, c, 0, nx)
            spread(m, c, 1, ny)
            spread(m, c, 3, nc)

    def forward_chunk(c):
        with scope("fw%d" % c):
            arrive(c, 0)
            if c % 2 == 0:
                spread(mx, c, 2, ny)
            spread(mx, c, 3, nc)
            arrive(c, 1)
            if c % 2 == 1:
                spread(my, c, 2, nx)
            spread(my, c, 3, nc)

    half = CHUNKS // 2

    def own_forward():
        with scope("ofw"):
            received(own.at[0], orecv.at[0])
            low = own.at[mx, pl.ds(0, half)]
            send(low, low, 6, orecv.at[2], ny)
            send(own.at[mx], own.at[mx], 6, orecv.at[3], nc)
            received(own.at[0], orecv.at[1])
            high = own.at[my, pl.ds(half, CHUNKS - half)]
            send(high, high, 6, orecv.at[2], nx)
            send(own.at[my], own.at[my], 6, orecv.at[3], nc)

    def own_finish():
        with scope("ofin"):
            received(own.at[0], orecv.at[2])
            send(own.at[mxy], own.at[mxy], 6, orecv.at[3], nc)

    def own_wait():
        with scope("ow"):
            received(own.at[pl.ds(0, 4)], orecv.at[3])

    def finish_chunk(c):
        with scope("fin%d" % c):
            arrive(c, 2)
            spread(mxy, c, 3, nc)

    def gate_up(c):
        with scope("guw%d" % c):
            arrive(c, 3)
        with scope("gu%d" % c):
            blocks = []
            for member in range(SPLIT):
                blocks.append(own[member, c].astype(F32))
                blocks += [arr[c, member, i].astype(F32) for i in range(groups - 1)]
            x = jnp.concatenate(blocks, axis=0).astype(BF16)
            g_part = jnp.dot(x, gw[c * cw : (c + 1) * cw], preferred_element_type=F32)
            u_part = jnp.dot(x, uw[c * cw : (c + 1) * cw], preferred_element_type=F32)
            if c == 0:
                acc[0] = g_part
                acc[1] = u_part
            else:
                acc[0] += g_part
                acc[1] += u_part

    pairs_n = heads // 2

    def ql(a, b):
        query_latents(a * pairs_n // 8, b * pairs_n // 8)

    seq = keys.shape[0] * keys.shape[1]
    scale = (nope + ropew) ** -0.5 * LOG2E
    vdim = vu.shape[2]

    def attend(first, last, most):
        size = min(hb, most)
        block = size * rows
        with scope("att%d" % first):
            @pl.loop(first // size, last // size)
            def _(b):
                q = qcat[pl.ds(pl.multiple_of(b * block, block), block)]
                kk = keys[...].reshape(seq, keys.shape[2])
                score = lax.dot_general(q, kk, NT, preferred_element_type=F32)
                top = jnp.max(score, axis=1, keepdims=True)
                expo = jnp.exp2((score - top) * scale)
                total = jnp.sum(expo, axis=1, keepdims=True)
                mixed = jnp.dot(expo.astype(BF16), kk[:, :lat], preferred_element_type=F32)
                mixed = (mixed / total).astype(BF16)
                for k in range(size):
                    h = b * size + k
                    value = jnp.dot(
                        mixed[k * rows : (k + 1) * rows], vu[h], preferred_element_type=F32
                    )
                    att_ref[:, pl.ds(pl.multiple_of(h * vdim, vdim), vdim)] = value.astype(BF16)

            cols = pl.ds(first * vdim, (last - first) * vdim)
            store(att_ref.at[:, cols], att_hbm.at[:, cols], 2)

    def far(fn, first):
        for s in range(first, groups):
            fn(s)

    ql(0, 4)
    start_chunk(0)
    key_a(0)
    own_forward()
    start_chunk(1)
    key_b(0)
    ql(4, 5)
    start_chunk(2)
    ql(5, 6)
    start_chunk(3)
    own_finish()
    forward_chunk(0)
    ql(6, 7)
    key_a(1)
    forward_chunk(1)
    ql(7, 8)
    forward_chunk(2)
    key_b(1)
    forward_chunk(3)
    finish_chunk(0)
    finish_chunk(1)
    key_a(2)
    finish_chunk(2)
    l_gw.wait()
    l_uw.wait()
    own_wait()
    gate_up(0)
    key_b(2)
    finish_chunk(3)
    gate_up(1)
    gate_up(2)
    gate_up(3)
    with scope("act"):
        gate_act = acc[0]
        hidden = (gate_act / (1.0 + jnp.exp(-gate_act)) * acc[1]).astype(BF16)
        l_dw.wait()

    def down(k):
        value = jnp.dot(hidden, dw[:, k * 2 * rw : (k + 1) * 2 * rw], preferred_element_type=F32)
        value = value.astype(BF16)
        for c in (2 * k, 2 * k + 1):
            start = (c % 2) * rw
            part[c] = value[:, start : start + rw].reshape(2, 2, 2, slots, rw)
            send(part.at[c, :, 1 - bc], r1.at[c], 2, rrecv.at[0, k], nc)

    def sum_cores(k):
        with scope("sc%d" % k):
            received(r1.at[pl.ds(0, 2)], rrecv.at[0, k])
            for c in (2 * k, 2 * k + 1):
                for a in range(2):
                    for b in range(2):
                        s1[c, a, b] = (part[c, a, bc, b].astype(F32) + r1[c, a, b].astype(F32)).astype(BF16)
            send(s1.at[2 * k, :, 1 - bx], r2.at[2 * k], 3, rrecv.at[1, k], nx)
            send(s1.at[2 * k + 1, 1 - by], r2.at[2 * k + 1], 3, rrecv.at[1, k], ny)

    def sum_first(k):
        with scope("sf%d" % k):
            received(r2.at[pl.ds(0, 2)], rrecv.at[1, k])
            for c in (2 * k, 2 * k + 1):
                for a in range(2):
                    mine = s1[c, a, bx] if c % 2 == 0 else s1[c, by, a]
                    s2[c, a] = (mine.astype(F32) + r2[c, a].astype(F32)).astype(BF16)
            send(s2.at[2 * k, 1 - by], r3.at[2 * k], 4, rrecv.at[2, k], ny)
            send(s2.at[2 * k + 1, 1 - bx], r3.at[2 * k + 1], 4, rrecv.at[2, k], nx)

    def sum_second(k):
        with scope("ss%d" % k):
            received(r3.at[pl.ds(0, 2)], rrecv.at[2, k])
            for c in (2 * k, 2 * k + 1):
                keep = by if c % 2 == 0 else bx
                total = s2[c, keep].astype(F32) + r3[c].astype(F32)
                for e in range(groups):
                    rbuf[c, e] = total[e * CAP : (e + 1) * CAP].astype(BF16)
                for i, o in enumerate(others):
                    send(rbuf.at[c, i + 1], res_hbm.at[c, g], 5, brecv.at[0], dev(o, m))
                store(rbuf.at[c, 0], res_hbm.at[c, g], 1)

    with scope("down"):
        for k in range(RCHUNKS // 2):
            down(k)
    far(key_a, 3)
    sum_cores(0)
    sum_cores(1)
    sum_cores(2)
    far(key_b, 3)
    with scope("vuw"):
        l_vu.wait()
    far(key_w, 0)
    attend(heads * 0 // 32, heads * 8 // 32, 8)
    sum_first(0)
    sum_cores(3)
    attend(heads * 8 // 32, heads * 12 // 32, 4)
    sum_first(1)
    attend(heads * 12 // 32, heads * 16 // 32, 4)
    sum_first(2)
    sum_second(0)
    attend(heads * 16 // 32, heads * 20 // 32, 4)
    sum_first(3)
    sum_second(1)
    sum_second(2)
    attend(heads * 20 // 32, heads * 24 // 32, 4)
    sum_second(3)
    attend(heads * 24 // 32, heads * 32 // 32, 8)

    with scope("z_res"):
        received(res_hbm.at[:, pl.ds(0, groups - 1)], brecv.at[0])
    with scope("z_sends"):
        sources = [
            outg.at[:, pl.ds(0, groups - 1)],
            arr.at[:, pl.ds(0, 7)],
            r1,
            r2,
            r3,
            rbuf.at[:, pl.ds(0, groups - 1)],
            own.at[pl.ds(0, 7)],
        ]
        for kind, source in enumerate(sources):
            rcopy(source, source, send_sem.at[kind], brecv.at[0], nx).wait_send()
        for s in range(groups):
            def sent_keys(like, way):
                rcopy(like, like, ksend.at[kslot(way, s)], krecv.at[0], nx).wait_send()

            if s == 0:
                sent_keys(kwhole(0), 1)
            if s < top_plane:
                @pl.when((g >= s) & (g < top_plane))
                def _():
                    sent_keys(kwhole(0), 0)
                    sent_keys(kwhole(0), 2)

            @functools.partial(guarded, s)
            def _():
                sent_keys(keys.at[pl.ds(0, 2), :, pl.ds(0, sent)], 3)

        pltpu.make_async_copy(wmix, wmix_hbm, store_sem.at[0]).wait()
        pltpu.make_async_copy(rbuf.at[:, 0], res_hbm.at[:, 0], store_sem.at[1]).wait()
        pltpu.make_async_copy(att_ref, att_hbm, store_sem.at[2]).wait()


def finish(res_hbm, wmix_hbm, att_hbm, rout_hbm, out_hbm, res, wmix, att, rout, sem):
    chunks, groups, _, cw = res.shape
    step = chunks // PIECES
    w_load = pltpu.make_async_copy(wmix_hbm, wmix, sem.at[0])
    w_load.start()
    loads = []
    for p in range(PIECES):
        piece = pl.ds(p * step, step)
        loads.append(pltpu.make_async_copy(res_hbm.at[piece], res.at[piece], sem.at[1 + p]))
        loads[p].start()
    a_load = pltpu.make_async_copy(att_hbm, att, sem.at[1 + PIECES])
    a_load.start()
    with scope("fw"):
        w_load.wait()
    stores = []
    for p in range(PIECES):
        with scope("fl%d" % p):
            loads[p].wait()
        for c in range(p * step, (p + 1) * step):
            blocks = [res[c, e].astype(F32) for e in range(groups)]
            block_rows = jnp.concatenate(blocks, axis=0).astype(BF16)
            tall = jnp.concatenate([block_rows] * 3, axis=0)
            rout[:, c * cw : (c + 1) * cw] = jnp.dot(
                wmix[:, : tall.shape[0]], tall, preferred_element_type=F32
            ).astype(BF16)
        cols = pl.ds(p * step * cw, step * cw)
        stores.append(
            pltpu.make_async_copy(rout.at[:, cols], rout_hbm.at[:, cols], sem.at[2 + PIECES + p])
        )
        stores[p].start()
        if p == 0:
            a_load.wait()
            a_store = pltpu.make_async_copy(att, out_hbm, sem.at[2 + 2 * PIECES])
            a_store.start()
    with scope("fz"):
        for cp in stores + [a_store]:
            cp.wait()


def local(n_ctx, n_sec, qn, qr, klat, krope, ku, vu, tok, ids, gates, gw, uw, dw):
    devices = n_ctx * n_sec
    groups = devices // SPLIT
    slots = groups * CAP
    rows = qn.shape[0]
    heads, lat, nope = ku.shape
    ropew = krope.shape[1]
    tokens, width = tok.shape
    cw = width // CHUNKS
    rw = width // RCHUNKS
    kw = lat + 2 * ropew + 128
    hb = 16 if n_ctx * rows <= 2048 else 1
    lanes = -(-3 * slots // 128) * 128
    dims = (groups, n_sec, rows, heads, lat, ropew, nope, hb)
    a = pl.BlockSpec(memory_space=pl.ANY)
    dma = pltpu.SemaphoreType.DMA
    out_width = heads * vu.shape[2]
    att, res, wmix = pl.pallas_call(
        functools.partial(kernel, dims),
        out_shape=(
            jax.ShapeDtypeStruct((rows, out_width), BF16),
            jax.ShapeDtypeStruct((RCHUNKS, groups, CAP, rw), BF16),
            jax.ShapeDtypeStruct((tokens, lanes), BF16),
        ),
        in_specs=[a] * 12,
        out_specs=(a, a, a),
        scratch_shapes=[
            pltpu.VMEM(ids.shape[::-1], ids.dtype),
            pltpu.VMEM(gates.shape[::-1], gates.dtype),
            pltpu.VMEM(krope.shape, BF16),
            pltpu.VMEM((tokens, lanes), BF16),
            pltpu.VMEM((rows, out_width), BF16),
            pltpu.VMEM(tok.shape, BF16),
            pltpu.VMEM(qn.shape, BF16),
            pltpu.VMEM(qr.shape, BF16),
            pltpu.VMEM(ku.shape, BF16),
            pltpu.VMEM(vu.shape, BF16),
            pltpu.VMEM(gw.shape, BF16),
            pltpu.VMEM(uw.shape, BF16),
            pltpu.VMEM(dw.shape, BF16),
            pltpu.VMEM((heads * rows, kw), BF16),
            pltpu.VMEM((n_ctx, rows, kw), BF16),
            pltpu.VMEM((CHUNKS, groups, CAP, cw), BF16),
            pltpu.VMEM((SPLIT, CHUNKS, CAP, cw), BF16),
            pltpu.VMEM((CHUNKS, SPLIT, groups - 1, CAP, cw), BF16),
            pltpu.VMEM((2, SPLIT * slots, gw.shape[1]), F32),
            pltpu.VMEM((RCHUNKS, 2, 2, 2, slots, rw), BF16),
            pltpu.VMEM((RCHUNKS, 2, 2, slots, rw), BF16),
            pltpu.VMEM((RCHUNKS, 2, 2, slots, rw), BF16),
            pltpu.VMEM((RCHUNKS, 2, slots, rw), BF16),
            pltpu.VMEM((RCHUNKS, 2, slots, rw), BF16),
            pltpu.VMEM((RCHUNKS, slots, rw), BF16),
            pltpu.VMEM((RCHUNKS, groups, CAP, rw), BF16),
            dma((11 + CHUNKS,)),
            dma((3,)),
            dma((7,)),
            dma((3 * groups + 1,)),
            dma((3 * groups + 1,)),
            dma((CHUNKS,)),
            dma((4,)),
            dma((CHUNKS, 4)),
            dma((3, RCHUNKS // 2)),
            dma((1,)),
        ],
        compiler_params=pltpu.CompilerParams(
            collective_id=0, has_side_effects=True, vmem_limit_bytes=67043328
        ),
    )(ids.T, gates.T, klat, krope, tok, qn, qr, ku, vu, gw, uw, dw)
    rout, att = pl.pallas_call(
        finish,
        out_shape=(jax.ShapeDtypeStruct(tok.shape, BF16), jax.ShapeDtypeStruct(att.shape, BF16)),
        in_specs=[a, a, a],
        out_specs=(a, a),
        scratch_shapes=[
            pltpu.VMEM(res.shape, BF16),
            pltpu.VMEM(wmix.shape, BF16),
            pltpu.VMEM(att.shape, BF16),
            pltpu.VMEM(tok.shape, BF16),
            dma((3 + 2 * PIECES,)),
        ],
    )(res, wmix, att)
    return att, rout


def solution(mesh):
    body = functools.partial(local, mesh.shape["ctx"], mesh.shape["sec"])
    both = ("ctx", "sec")
    return jax.shard_map(
        body,
        mesh=mesh,
        in_specs=(
            P("ctx", "sec"),
            P("ctx", "sec"),
            P("ctx", None),
            P("ctx", None),
            P("sec", None, None),
            P("sec", None, None),
            P(both, None),
            P(both, None),
            P(both, None),
            P(None, both),
            P(None, both),
            P(both, None),
        ),
        out_specs=(P("ctx", "sec"), P(both, None)),
        check_vma=False,
    )
```

```python
import functools

import jax
import jax.numpy as jnp
from jax import lax
from jax.experimental import pallas as pl
from jax.experimental.pallas import tpu as pltpu
from jax.sharding import PartitionSpec as P

CAP = 4
SPLIT = 8
CHUNKS = 4
RCHUNKS = 8
PIECES = 2
LOG2E = 1.4426950408889634
MESH_ID = pl.DeviceIdType.MESH
F32 = jnp.float32
BF16 = jnp.bfloat16
NT = (((1,), (1,)), ((), ()))
scope = jax.named_scope


def kernel(
    dims,
    ids_hbm,
    gates_hbm,
    klat_hbm,
    krope_hbm,
    tok_hbm,
    qn_hbm,
    qr_hbm,
    ku_hbm,
    vu_hbm,
    gw_hbm,
    uw_hbm,
    dw_hbm,
    att_hbm,
    res_hbm,
    wmix_hbm,
    ids_ref,
    gates_ref,
    krope_ref,
    wmix,
    att_ref,
    tok,
    qn,
    qr,
    ku,
    vu,
    gw,
    uw,
    dw,
    qcat,
    keys,
    outg,
    own,
    arr,
    acc,
    part,
    r1,
    s1,
    r2,
    s2,
    r3,
    rbuf,
    load_sem,
    store_sem,
    send_sem,
    ksend,
    krecv,
    zrecv,
    orecv,
    arecv,
    rrecv,
    brecv,
):
    groups, n_sec, rows, heads, lat, ropew, nope, hb = dims
    slots = groups * CAP
    width = tok.shape[1]
    cw = width // CHUNKS
    rw = width // RCHUNKS
    tokens = tok.shape[0]
    sent = lat + 2 * ropew
    ctx = lax.axis_index("ctx")
    sec = lax.axis_index("sec")
    me = ctx * n_sec + sec
    g = me // SPLIT
    m = lax.rem(me, SPLIT)
    bx = lax.rem(m, 2)
    bc = lax.rem(m // 2, 2)
    by = m // 4
    mx = m + 1 - 2 * bx
    mc = m + 2 - 4 * bc
    my = m + 4 - 8 * by
    mxy = mx + my - m

    def dev(group, member):
        index = group * SPLIT + member
        return (index // n_sec, lax.rem(index, n_sec))


    def rcopy(src, dst, ss, rs, target):
        return pltpu.make_async_remote_copy(
            src_ref=src, dst_ref=dst, send_sem=ss, recv_sem=rs,
            device_id=target, device_id_type=MESH_ID,
        )

    def send(src, dst, kind, rs, target):
        rcopy(src, dst, send_sem.at[kind], rs, target).start()

    def received(like, rs):
        rcopy(like, like, send_sem.at[0], rs, nx).wait_recv()

    def store(src, dst, kind):
        pltpu.make_async_copy(src, dst, store_sem.at[kind]).start()

    nx, nc, ny = dev(g, mx), dev(g, mc), dev(g, my)
    others = [lax.rem(g + step, groups) for step in range(1, groups)]
    every = [g] + others

    barrier = pltpu.get_barrier_semaphore()
    for target in [dev(o, m) for o in others] + [nx, nc, ny]:
        pl.semaphore_signal(barrier, inc=1, device_id=target, device_id_type=MESH_ID)

    own_keys = keys.at[ctx]
    pairs = [
        (ids_hbm, ids_ref), (gates_hbm, gates_ref), (qn_hbm, qn), (qr_hbm, qr), (ku_hbm, ku),
        (gw_hbm, gw), (uw_hbm, uw), (dw_hbm, dw), (vu_hbm, vu),
        (klat_hbm, own_keys.at[:, pl.ds(0, lat)]), (krope_hbm, krope_ref),
    ]
    loads = [pltpu.make_async_copy(a, b, load_sem.at[i]) for i, (a, b) in enumerate(pairs)]
    l_ids, l_gates, l_qn, l_qr, l_ku, l_gw, l_uw, l_dw, l_vu, l_klat, l_krope = loads
    l_ids.start()
    l_gates.start()
    tok_loads = []
    for c in range(CHUNKS):
        cols = pl.ds(c * cw, cw)
        tok_loads.append(
            pltpu.make_async_copy(
                tok_hbm.at[:, cols], tok.at[:, cols], load_sem.at[len(loads) + c]
            )
        )
        tok_loads[c].start()
    l_klat.start()
    l_krope.start()

    def kwhole(shard):
        return keys.at[shard, :, pl.ds(0, sent)]

    def kshard(group, member):
        return (group * SPLIT + member) // n_sec

    def kslot(way, s):
        return (groups + 1, groups, 2 * groups + 1, 0)[way] + s

    def whole(group, member, way, s, target, rs=None):
        piece = kwhole(kshard(group, member))
        rcopy(piece, piece, ksend.at[kslot(way, s)], krecv.at[kslot(way, s if rs is None else rs)], target).start()

    up = dev(lax.rem(g + 1, groups), m)
    top_plane = groups - 1

    def guarded(s, fn):
        if s == 0:
            fn()
        else:
            pl.when(g >= s)(fn)

    def key_up(s, member, way):
        if s >= top_plane:
            return
        cond = g < top_plane if s == 0 else (g >= s) & (g < top_plane)

        @pl.when(cond)
        def _():
            whole(g - s, member, way, s, up, s + 1)

    def key_own():
        whole(g, m, 1, 0, ny)
        whole(g, m, 3, 0, nc)

    def key_pass(s, member, way):
        with scope("kp%d_%d" % (s, way)):
            if s == 0 and way == 0:
                key_up(0, m, 0)
                return

            @functools.partial(guarded, s)
            def _():
                received(kwhole(0), krecv.at[kslot(1 if s == 0 else way, s)])

            key_up(s, member, way)

            @functools.partial(guarded, s)
            def _():
                whole(g - s, member, 3, s, nc)

    def key_a(s):
        key_pass(s, m, 0)

    def key_b(s):
        key_pass(s, my, 2)

    def key_w(s):
        with scope("kw%d" % s):
            @functools.partial(guarded, s)
            def _():
                received(keys.at[pl.ds(0, 2), :, pl.ds(0, sent)], krecv.at[kslot(3, s)])

    with scope("a_sel"):
        lanes = wmix.shape[1]
        row = lax.broadcasted_iota(jnp.int32, (lanes, tokens), 0)
        slot = row & (slots - 1)
        expert = slot // CAP
        matches = jnp.zeros((lanes, tokens), F32)
        gate = jnp.zeros((lanes, tokens), F32)
        l_ids.wait()
        l_gates.wait()
        for load in (l_qn, l_qr, l_ku):
            load.start()
        for k in range(ids_ref.shape[0]):
            hit = ids_ref[k : k + 1, :] == expert
            matches = jnp.where(hit, 1.0, matches)
            gate = gate + jnp.where(hit, gates_ref[k : k + 1, :], 0.0)
        earlier = (
            lax.broadcasted_iota(jnp.int32, (tokens, tokens), 0)
            < lax.broadcasted_iota(jnp.int32, (tokens, tokens), 1)
        )
        rank = jnp.dot(
            matches.astype(BF16), jnp.where(earlier, 1.0, 0.0).astype(BF16), preferred_element_type=F32
        )
        chosen = jnp.where(rank == (slot & (CAP - 1)).astype(F32), matches, 0.0)
        picker = chosen[:slots].astype(BF16)

    with scope("b_pick"):
        for c in range(CHUNKS):
            tok_loads[c].wait()
            picked = jnp.dot(picker, tok[:, c * cw : (c + 1) * cw], preferred_element_type=F32)
            for e in range(groups):
                outg[c, e] = picked[e * CAP : (e + 1) * CAP].astype(BF16)
        l_klat.wait()
        l_krope.wait()
        own_keys[:, lat:sent] = jnp.concatenate([krope_ref[...], krope_ref[...]], axis=1)

    with scope("c_barrier"):
        pl.semaphore_wait(barrier, 3 + len(others))

    with scope("d_zsend"):
        for c in range(CHUNKS):
            for i, o in enumerate(others):
                send(outg.at[c, o], arr.at[c, m, groups - 2 - i], 0, zrecv.at[c], dev(o, m))
        own[m] = outg[:, g]
        for way, target in enumerate((nx, ny)):
            send(own.at[m], own.at[m], 6, orecv.at[way], target)
        send(own.at[m], own.at[m], 6, orecv.at[3], nc)
        key_own()

    with scope("e_wmix"):
        weight = chosen * gate
        w1 = weight.astype(BF16).astype(F32)
        w2 = (weight - w1).astype(BF16).astype(F32)
        w3 = weight - w1 - w2
        wmix[...] = jnp.where(
            row < slots, w1, jnp.where(row < 2 * slots, w2, jnp.where(row < 3 * slots, w3, 0.0))
        ).T.astype(BF16)
        store(wmix, wmix_hbm, 0)

        maskw = keys.shape[2] - sent

        @pl.loop(0, keys.shape[0])
        def _(shard):
            key_place = shard * rows + lax.broadcasted_iota(jnp.int32, (rows, maskw), 0)
            query = lax.broadcasted_iota(jnp.int32, (rows, maskw), 1)
            hidden_key = (key_place > ctx * rows + query) & (query < rows)
            keys[shard, :, sent:] = jnp.where(hidden_key, -1e30, 0.0).astype(BF16)

        unit = jnp.where(
            lax.broadcasted_iota(jnp.int32, (rows, maskw), 0)
            == lax.broadcasted_iota(jnp.int32, (rows, maskw), 1),
            1.0,
            0.0,
        ).astype(BF16)

    per = SPLIT // n_sec
    with scope("zero"):
        for s in range(1, groups):
            @pl.when(g + s < groups)
            def _():
                keys[pl.ds((g + s) * per, per), :, :sent] = jnp.zeros((per, rows, sent), BF16)

    with scope("f_loads"):
        l_qn.wait()
        l_qr.wait()
        l_ku.wait()
        for load in (l_gw, l_uw, l_dw, l_vu):
            load.start()

    def query_latents(first, last):
        with scope("ql"):
            @pl.loop(first, last)
            def _(p):
                rope = qr[:, pl.ds(pl.multiple_of(p * 2 * ropew, 2 * ropew), 2 * ropew)]
                low = lax.broadcasted_iota(jnp.int32, rope.shape, 1) < ropew
                for k in range(2):
                    h = p * 2 + k
                    q = qn[:, pl.ds(pl.multiple_of(h * nope, nope), nope)]
                    latent = lax.dot_general(q, ku[h], NT, preferred_element_type=F32)
                    place = pl.ds(pl.multiple_of(h * rows, rows), rows)
                    qcat[place, :lat] = latent.astype(BF16)
                    keep = low if k == 0 else jnp.logical_not(low)
                    qcat[place, lat:sent] = jnp.where(keep, rope.astype(F32), 0.0).astype(BF16)
                    qcat[place, sent:] = unit

    def spread(member, c, way, target):
        piece = arr.at[c, member]
        send(piece, piece, 1, arecv.at[c, way], target)

    def arrive(c, way):
        received(arr.at[c, 0] if way < 3 else arr.at[c, pl.ds(0, 4)], arecv.at[c, way])

    def start_chunk(c):
        with scope("s%d" % c):
            received(arr.at[c, 0], zrecv.at[c])
            spread(m, c, 0, nx)
            spread(m, c, 1, ny)
            spread(m, c, 3, nc)

    def forward_chunk(c):
        with scope("fw%d" % c):
            arrive(c, 0)
            if c % 2 == 0:
                spread(mx, c, 2, ny)
            spread(mx, c, 3, nc)
            arrive(c, 1)
            if c % 2 == 1:
                spread(my, c, 2, nx)
            spread(my, c, 3, nc)

    half = CHUNKS // 2

    def own_forward():
        with scope("ofw"):
            received(own.at[0], orecv.at[0])
            low = own.at[mx, pl.ds(0, half)]
            send(low, low, 6, orecv.at[2], ny)
            send(own.at[mx], own.at[mx], 6, orecv.at[3], nc)
            received(own.at[0], orecv.at[1])
            high = own.at[my, pl.ds(half, CHUNKS - half)]
            send(high, high, 6, orecv.at[2], nx)
            send(own.at[my], own.at[my], 6, orecv.at[3], nc)

    def own_finish():
        with scope("ofin"):
            received(own.at[0], orecv.at[2])
            send(own.at[mxy], own.at[mxy], 6, orecv.at[3], nc)

    def own_wait():
        with scope("ow"):
            received(own.at[pl.ds(0, 4)], orecv.at[3])

    def finish_chunk(c):
        with scope("fin%d" % c):
            arrive(c, 2)
            spread(mxy, c, 3, nc)

    def gate_up(c):
        with scope("guw%d" % c):
            arrive(c, 3)
        with scope("gu%d" % c):
            blocks = []
            for member in range(SPLIT):
                blocks.append(own[member, c].astype(F32))
                blocks += [arr[c, member, i].astype(F32) for i in range(groups - 1)]
            x = jnp.concatenate(blocks, axis=0).astype(BF16)
            g_part = jnp.dot(x, gw[c * cw : (c + 1) * cw], preferred_element_type=F32)
            u_part = jnp.dot(x, uw[c * cw : (c + 1) * cw], preferred_element_type=F32)
            if c == 0:
                acc[0] = g_part
                acc[1] = u_part
            else:
                acc[0] += g_part
                acc[1] += u_part

    pairs_n = heads // 2

    def ql(a, b):
        query_latents(a * pairs_n // 8, b * pairs_n // 8)

    seq = keys.shape[0] * keys.shape[1]
    scale = (nope + ropew) ** -0.5 * LOG2E
    vdim = vu.shape[2]

    def attend(first, last, most):
        size = min(hb, most)
        block = size * rows
        with scope("att%d" % first):
            @pl.loop(first // size, last // size)
            def _(b):
                q = qcat[pl.ds(pl.multiple_of(b * block, block), block)]
                kk = keys[...].reshape(seq, keys.shape[2])
                score = lax.dot_general(q, kk, NT, preferred_element_type=F32)
                top = jnp.max(score, axis=1, keepdims=True)
                expo = jnp.exp2((score - top) * scale)
                total = jnp.sum(expo, axis=1, keepdims=True)
                mixed = jnp.dot(expo.astype(BF16), kk[:, :lat], preferred_element_type=F32)
                mixed = (mixed / total).astype(BF16)
                for k in range(size):
                    h = b * size + k
                    value = jnp.dot(
                        mixed[k * rows : (k + 1) * rows], vu[h], preferred_element_type=F32
                    )
                    att_ref[:, pl.ds(pl.multiple_of(h * vdim, vdim), vdim)] = value.astype(BF16)

            cols = pl.ds(first * vdim, (last - first) * vdim)
            store(att_ref.at[:, cols], att_hbm.at[:, cols], 2)

    def far(fn, first):
        for s in range(first, groups):
            fn(s)

    ql(0, 4)
    start_chunk(0)
    key_a(0)
    own_forward()
    start_chunk(1)
    key_b(0)
    ql(4, 5)
    start_chunk(2)
    ql(5, 6)
    start_chunk(3)
    own_finish()
    forward_chunk(0)
    ql(6, 7)
    key_a(1)
    forward_chunk(1)
    ql(7, 8)
    forward_chunk(2)
    key_b(1)
    forward_chunk(3)
    finish_chunk(0)
    finish_chunk(1)
    key_a(2)
    finish_chunk(2)
    l_gw.wait()
    l_uw.wait()
    own_wait()
    gate_up(0)
    key_b(2)
    finish_chunk(3)
    gate_up(1)
    gate_up(2)
    gate_up(3)
    with scope("act"):
        gate_act = acc[0]
        hidden = (gate_act / (1.0 + jnp.exp(-gate_act)) * acc[1]).astype(BF16)
        l_dw.wait()

    def down(k):
        value = jnp.dot(hidden, dw[:, k * 2 * rw : (k + 1) * 2 * rw], preferred_element_type=F32)
        value = value.astype(BF16)
        for c in (2 * k, 2 * k + 1):
            start = (c % 2) * rw
            part[c] = value[:, start : start + rw].reshape(2, 2, 2, slots, rw)
            send(part.at[c, :, 1 - bc], r1.at[c], 2, rrecv.at[0, k], nc)

    def sum_cores(k):
        with scope("sc%d" % k):
            received(r1.at[pl.ds(0, 2)], rrecv.at[0, k])
            for c in (2 * k, 2 * k + 1):
                for a in range(2):
                    for b in range(2):
                        s1[c, a, b] = (part[c, a, bc, b].astype(F32) + r1[c, a, b].astype(F32)).astype(BF16)
            send(s1.at[2 * k, :, 1 - bx], r2.at[2 * k], 3, rrecv.at[1, k], nx)
            send(s1.at[2 * k + 1, 1 - by], r2.at[2 * k + 1], 3, rrecv.at[1, k], ny)

    def sum_first(k):
        with scope("sf%d" % k):
            received(r2.at[pl.ds(0, 2)], rrecv.at[1, k])
            for c in (2 * k, 2 * k + 1):
                for a in range(2):
                    mine = s1[c, a, bx] if c % 2 == 0 else s1[c, by, a]
                    s2[c, a] = (mine.astype(F32) + r2[c, a].astype(F32)).astype(BF16)
            send(s2.at[2 * k, 1 - by], r3.at[2 * k], 4, rrecv.at[2, k], ny)
            send(s2.at[2 * k + 1, 1 - bx], r3.at[2 * k + 1], 4, rrecv.at[2, k], nx)

    def sum_second(k):
        with scope("ss%d" % k):
            received(r3.at[pl.ds(0, 2)], rrecv.at[2, k])
            for c in (2 * k, 2 * k + 1):
                keep = by if c % 2 == 0 else bx
                total = s2[c, keep].astype(F32) + r3[c].astype(F32)
                for e in range(groups):
                    rbuf[c, e] = total[e * CAP : (e + 1) * CAP].astype(BF16)
                for i, o in reversed(list(enumerate(others))):
                    send(rbuf.at[c, i + 1], res_hbm.at[c, g], 5, brecv.at[0], dev(o, m))
                store(rbuf.at[c, 0], res_hbm.at[c, g], 1)

    with scope("down"):
        for k in range(RCHUNKS // 2):
            down(k)
    far(key_a, 3)
    sum_cores(0)
    sum_cores(1)
    sum_cores(2)
    sum_cores(3)
    far(key_b, 3)
    with scope("vuw"):
        l_vu.wait()
    far(key_w, 0)
    attend(heads * 0 // 32, heads * 8 // 32, 8)
    sum_first(0)
    attend(heads * 8 // 32, heads * 12 // 32, 4)
    sum_first(1)
    attend(heads * 12 // 32, heads * 16 // 32, 4)
    sum_first(2)
    sum_second(0)
    sum_first(3)
    sum_second(1)
    attend(heads * 16 // 32, heads * 20 // 32, 4)
    sum_second(2)
    sum_second(3)
    attend(heads * 20 // 32, heads * 32 // 32, 4)

    with scope("z_res"):
        received(res_hbm.at[:, pl.ds(0, groups - 1)], brecv.at[0])
    with scope("z_sends"):
        sources = [
            outg.at[:, pl.ds(0, groups - 1)],
            arr.at[:, pl.ds(0, 7)],
            r1,
            r2,
            r3,
            rbuf.at[:, pl.ds(0, groups - 1)],
            own.at[pl.ds(0, 7)],
        ]
        for kind, source in enumerate(sources):
            rcopy(source, source, send_sem.at[kind], brecv.at[0], nx).wait_send()
        for s in range(groups):
            def sent_keys(like, way):
                rcopy(like, like, ksend.at[kslot(way, s)], krecv.at[0], nx).wait_send()

            if s == 0:
                sent_keys(kwhole(0), 1)
            if s < top_plane:
                @pl.when((g >= s) & (g < top_plane))
                def _():
                    sent_keys(kwhole(0), 0)
                    sent_keys(kwhole(0), 2)

            @functools.partial(guarded, s)
            def _():
                sent_keys(keys.at[pl.ds(0, 2), :, pl.ds(0, sent)], 3)

        pltpu.make_async_copy(wmix, wmix_hbm, store_sem.at[0]).wait()
        pltpu.make_async_copy(rbuf.at[:, 0], res_hbm.at[:, 0], store_sem.at[1]).wait()
        pltpu.make_async_copy(att_ref, att_hbm, store_sem.at[2]).wait()


def finish(res_hbm, wmix_hbm, att_hbm, rout_hbm, out_hbm, res, wmix, att, rout, sem):
    chunks, groups, _, cw = res.shape
    step = chunks // PIECES
    w_load = pltpu.make_async_copy(wmix_hbm, wmix, sem.at[0])
    w_load.start()
    loads = []
    for p in range(PIECES):
        piece = pl.ds(p * step, step)
        loads.append(pltpu.make_async_copy(res_hbm.at[piece], res.at[piece], sem.at[1 + p]))
        loads[p].start()
    a_load = pltpu.make_async_copy(att_hbm, att, sem.at[1 + PIECES])
    a_load.start()
    with scope("fw"):
        w_load.wait()
    stores = []
    for p in range(PIECES):
        with scope("fl%d" % p):
            loads[p].wait()
        for c in range(p * step, (p + 1) * step):
            blocks = [res[c, e].astype(F32) for e in range(groups)]
            block_rows = jnp.concatenate(blocks, axis=0).astype(BF16)
            tall = jnp.concatenate([block_rows] * 3, axis=0)
            rout[:, c * cw : (c + 1) * cw] = jnp.dot(
                wmix[:, : tall.shape[0]], tall, preferred_element_type=F32
            ).astype(BF16)
        cols = pl.ds(p * step * cw, step * cw)
        stores.append(
            pltpu.make_async_copy(rout.at[:, cols], rout_hbm.at[:, cols], sem.at[2 + PIECES + p])
        )
        stores[p].start()
        if p == 0:
            a_load.wait()
            a_store = pltpu.make_async_copy(att, out_hbm, sem.at[2 + 2 * PIECES])
            a_store.start()
    with scope("fz"):
        for cp in stores + [a_store]:
            cp.wait()


def local(n_ctx, n_sec, qn, qr, klat, krope, ku, vu, tok, ids, gates, gw, uw, dw):
    devices = n_ctx * n_sec
    groups = devices // SPLIT
    slots = groups * CAP
    rows = qn.shape[0]
    heads, lat, nope = ku.shape
    ropew = krope.shape[1]
    tokens, width = tok.shape
    cw = width // CHUNKS
    rw = width // RCHUNKS
    kw = lat + 2 * ropew + 128
    hb = 16 if n_ctx * rows <= 2048 else 1
    lanes = -(-3 * slots // 128) * 128
    dims = (groups, n_sec, rows, heads, lat, ropew, nope, hb)
    a = pl.BlockSpec(memory_space=pl.ANY)
    dma = pltpu.SemaphoreType.DMA
    out_width = heads * vu.shape[2]
    att, res, wmix = pl.pallas_call(
        functools.partial(kernel, dims),
        out_shape=(
            jax.ShapeDtypeStruct((rows, out_width), BF16),
            jax.ShapeDtypeStruct((RCHUNKS, groups, CAP, rw), BF16),
            jax.ShapeDtypeStruct((tokens, lanes), BF16),
        ),
        in_specs=[a] * 12,
        out_specs=(a, a, a),
        scratch_shapes=[
            pltpu.VMEM(ids.shape[::-1], ids.dtype),
            pltpu.VMEM(gates.shape[::-1], gates.dtype),
            pltpu.VMEM(krope.shape, BF16),
            pltpu.VMEM((tokens, lanes), BF16),
            pltpu.VMEM((rows, out_width), BF16),
            pltpu.VMEM(tok.shape, BF16),
            pltpu.VMEM(qn.shape, BF16),
            pltpu.VMEM(qr.shape, BF16),
            pltpu.VMEM(ku.shape, BF16),
            pltpu.VMEM(vu.shape, BF16),
            pltpu.VMEM(gw.shape, BF16),
            pltpu.VMEM(uw.shape, BF16),
            pltpu.VMEM(dw.shape, BF16),
            pltpu.VMEM((heads * rows, kw), BF16),
            pltpu.VMEM((n_ctx, rows, kw), BF16),
            pltpu.VMEM((CHUNKS, groups, CAP, cw), BF16),
            pltpu.VMEM((SPLIT, CHUNKS, CAP, cw), BF16),
            pltpu.VMEM((CHUNKS, SPLIT, groups - 1, CAP, cw), BF16),
            pltpu.VMEM((2, SPLIT * slots, gw.shape[1]), F32),
            pltpu.VMEM((RCHUNKS, 2, 2, 2, slots, rw), BF16),
            pltpu.VMEM((RCHUNKS, 2, 2, slots, rw), BF16),
            pltpu.VMEM((RCHUNKS, 2, 2, slots, rw), BF16),
            pltpu.VMEM((RCHUNKS, 2, slots, rw), BF16),
            pltpu.VMEM((RCHUNKS, 2, slots, rw), BF16),
            pltpu.VMEM((RCHUNKS, slots, rw), BF16),
            pltpu.VMEM((RCHUNKS, groups, CAP, rw), BF16),
            dma((11 + CHUNKS,)),
            dma((3,)),
            dma((7,)),
            dma((3 * groups + 1,)),
            dma((3 * groups + 1,)),
            dma((CHUNKS,)),
            dma((4,)),
            dma((CHUNKS, 4)),
            dma((3, RCHUNKS // 2)),
            dma((1,)),
        ],
        compiler_params=pltpu.CompilerParams(
            collective_id=0, has_side_effects=True, vmem_limit_bytes=67043328
        ),
    )(ids.T, gates.T, klat, krope, tok, qn, qr, ku, vu, gw, uw, dw)
    rout, att = pl.pallas_call(
        finish,
        out_shape=(jax.ShapeDtypeStruct(tok.shape, BF16), jax.ShapeDtypeStruct(att.shape, BF16)),
        in_specs=[a, a, a],
        out_specs=(a, a),
        scratch_shapes=[
            pltpu.VMEM(res.shape, BF16),
            pltpu.VMEM(wmix.shape, BF16),
            pltpu.VMEM(att.shape, BF16),
            pltpu.VMEM(tok.shape, BF16),
            dma((3 + 2 * PIECES,)),
        ],
    )(res, wmix, att)
    return att, rout


def solution(mesh):
    body = functools.partial(local, mesh.shape["ctx"], mesh.shape["sec"])
    both = ("ctx", "sec")
    return jax.shard_map(
        body,
        mesh=mesh,
        in_specs=(
            P("ctx", "sec"),
            P("ctx", "sec"),
            P("ctx", None),
            P("ctx", None),
            P("sec", None, None),
            P("sec", None, None),
            P(both, None),
            P(both, None),
            P(both, None),
            P(None, both),
            P(None, both),
            P(both, None),
        ),
        out_specs=(P("ctx", "sec"), P(both, None)),
        check_vma=False,
    )
```
